128 devices in a mesh: lat: 8 (over z, x_lo), lon: 16 (over y, x_hi, core).
Axes of the slice: x: 4 (x_hi: 2, x_lo: 2; x = x_hi * 2 + x_lo), y: 4, z: 4, core: 2. Of those that a mesh axis runs over, the one named last changes fastest.
Arguments:
- state: float32 [2, 6144, 12288], P(None, 'lat', 'lon'), may hold values from -6 to 6
- direction: float32 [2, 6144, 12288], P(None, 'lat', 'lon'), may hold values from -6 to 6
- diffusivity: bfloat16 [6144, 12288], P('lat', 'lon'), may hold values from 0.29882812 to 3
- inverses: bfloat16 [768, 8, 8, 24, 256], P(('lat', 'lon')), may hold values from -1.5 to 3
Outputs:
- preconditioned: float32 [2, 6144, 12288], P(None, 'lat', 'lon')
- jacobian_product: float32 [2, 6144, 12288], P(None, 'lat', 'lon')
The draws below stay inside these ranges and needn't reach their ends.
All inputs are finite; a program needn't handle non-finite values.
Results may differ from the reference program's by a relative error of at most 0.0003.
Values sent between devices are 32-bit elements; how exact they have to be, the bound alone decides.
A program may use at most 128 MiB of HBM per device.

```python
import math
import jax
import jax.numpy as jnp
from jax import lax

CLAT = 768
NLAT = 6144
NLON = 12288
LEV = 2
ZSPLIT = 24
HALFZ = 256
BLK = 8


def draw_inverses(key, part):
    shape = (NLAT // BLK, BLK, BLK, ZSPLIT, HALFZ)
    diag_key, noise_key = jax.random.split(jax.random.fold_in(key, 11))
    lowest, highest = (0.2, 2.0)
    scales = jnp.exp(jax.random.uniform(diag_key, (NLAT // BLK, BLK, 1, ZSPLIT, HALFZ), jnp.float32, jnp.log(lowest), jnp.log(highest)))
    noise = jnp.clip(jax.random.normal(noise_key, shape, jnp.float32), -4.0, 4.0)
    identity = (jnp.arange(BLK)[:, None] == jnp.arange(BLK)[None, :]).astype(jnp.float32)[None, :, :, None, None]
    values = scales * (identity + 0.12 * noise * (1.0 - identity))
    return values.astype(jnp.bfloat16)


def levels(stream_key, shape, cuts, smallest, high):
    def one(dim, blocks):
        steps = jax.random.uniform(jax.random.fold_in(jax.random.fold_in(stream_key, 6), dim), (blocks,), jnp.float32, smallest / len(cuts), high / len(cuts))
        return jnp.repeat(jnp.exp(steps), shape[dim] // blocks).reshape((-1,) + (1,) * (len(shape) - dim - 1))

    loudness = one(*cuts[0])
    for cut in cuts[1:]:
        loudness = loudness * one(*cut)
    return loudness


def centred(stream_key, extent, deviation, most, cuts=(), kind=jnp.bfloat16):
    loudness = levels(stream_key, extent, cuts, -0.22, 0.18) if cuts else 1.0
    drawn = jax.random.normal(stream_key, extent, jnp.float32) * deviation * loudness
    return jnp.minimum(jnp.maximum(drawn, -most), most).astype(kind)


def setup_inputs(seed: int = 0) -> dict:
    key_of = jax.random.split(jax.random.key(seed), 5)
    state = centred(key_of[0], (LEV, NLAT, NLON), 1.0, 6.0, ((1, 8), (2, 16)), jnp.float32)
    direction = centred(key_of[1], (LEV, NLAT, NLON), 1.0, 6.0, ((1, 8), (2, 16)), jnp.float32)
    diffusivity = jnp.clip(jnp.exp(math.log(3.0) - 2.306499 * jax.random.uniform(key_of[2], (NLAT, NLON), jnp.float32) ** levels(key_of[2], (NLAT, NLON), ((0, 8), (1, 16)), -0.2, 0.2)), 0.29882812, 3.0).astype(jnp.bfloat16)
    inverses = draw_inverses(jax.random.fold_in(key_of[4], 71), 0)
    return dict(state=state, direction=direction, diffusivity=diffusivity, inverses=inverses)


zonal_tau = 0.1
merid_tau = 0.5
zonal_cap = 16.0
quad_coef = 0.25
step_size = 0.01


def lat_geometry(first_row, count, total):
    rows = (first_row + jnp.arange(count, dtype=jnp.int32)).astype(jnp.float32)
    limit = jnp.float32(total)
    cell_cos = jnp.sin(jnp.pi * (rows + 0.5) / limit)
    low_face = rows
    high_face = rows + 1.0
    face_low = jnp.where((low_face > 0.0) & (low_face < limit), jnp.sin(jnp.pi * low_face / limit), 0.0)
    face_high = jnp.where(high_face < limit, jnp.sin(jnp.pi * high_face / limit), 0.0)
    zonal_factor = jnp.minimum(1.0 / (cell_cos * cell_cos), zonal_cap)
    return cell_cos[:, None], face_low[:, None], face_high[:, None], zonal_factor[:, None]


def tendency(padded, kappa_field, cell_cos, face_low, face_high, zonal_factor):
    centre = padded[:, 1:-1, 1:-1]
    east_cell = padded[:, 1:-1, 2:]
    west_cell = padded[:, 1:-1, :-2]
    north_cell = padded[:, 2:, 1:-1]
    south_cell = padded[:, :-2, 1:-1]
    east_flux = zonal_tau * zonal_factor * (1.0 + quad_coef * jnp.square(0.5 * (centre + east_cell))) * (east_cell - centre)
    west_flux = zonal_tau * zonal_factor * (1.0 + quad_coef * jnp.square(0.5 * (centre + west_cell))) * (centre - west_cell)
    north_flux = merid_tau * face_high * (1.0 + quad_coef * jnp.square(0.5 * (centre + north_cell))) * (north_cell - centre)
    south_flux = merid_tau * face_low * (1.0 + quad_coef * jnp.square(0.5 * (centre + south_cell))) * (centre - south_cell)
    spread = (east_flux - west_flux) + (north_flux - south_flux) / cell_cos
    return centre - kappa_field * spread


def extend(field):
    field = jnp.concatenate([field[:, :, -1:], field, field[:, :, :1]], 2)
    return jnp.pad(field, ((0, 0), (1, 1), (0, 0)))


def reference(state, direction, diffusivity, inverses):
    bands = NLAT // CLAT
    band_ids = jnp.arange(bands, dtype=jnp.int32)

    def precondition(band):
        rows_in = lax.dynamic_slice_in_dim(direction, band * CLAT, CLAT, 1)
        blocks = lax.dynamic_slice_in_dim(inverses, band * (CLAT // BLK), CLAT // BLK, 0).astype(jnp.float32)
        spectrum = jnp.fft.rfft(rows_in, axis=-1)[..., : NLON // 2]
        spectrum = spectrum.reshape(LEV, CLAT // BLK, BLK, HALFZ, ZSPLIT)
        spectrum = jnp.swapaxes(spectrum, 3, 4)
        real_part = jnp.einsum("brskq,lbskq->lbrkq", blocks, spectrum.real.astype(jnp.float32))
        imag_part = jnp.einsum("brskq,lbskq->lbrkq", blocks, spectrum.imag.astype(jnp.float32))
        solved = lax.complex(real_part, imag_part)
        solved = jnp.swapaxes(solved, 3, 4).reshape(LEV, CLAT, NLON // 2)
        solved = jnp.concatenate([solved, jnp.zeros((LEV, CLAT, 1), solved.dtype)], 2)
        return jnp.fft.irfft(solved, n=NLON, axis=-1).astype(jnp.float32)

    pieces = lax.map(precondition, band_ids)
    preconditioned = jnp.transpose(pieces, (1, 0, 2, 3)).reshape(LEV, NLAT, NLON)
    state_pad = extend(state)
    field_pad = extend(preconditioned)

    def product(band):
        base_pad = lax.dynamic_slice_in_dim(state_pad, band * CLAT, CLAT + 2, 1)
        moved_pad = lax.dynamic_slice_in_dim(field_pad, band * CLAT, CLAT + 2, 1)
        kappa_field = lax.dynamic_slice_in_dim(diffusivity, band * CLAT, CLAT, 0).astype(jnp.float32)
        geometry = lat_geometry(band * CLAT, CLAT, NLAT)
        base = tendency(base_pad, kappa_field, *geometry)
        moved = tendency(base_pad + step_size * moved_pad, kappa_field, *geometry)
        return (moved - base) / step_size

    parts = lax.map(product, band_ids)
    jacobian_product = jnp.transpose(parts, (1, 0, 2, 3)).reshape(LEV, NLAT, NLON)
    return preconditioned, jacobian_product
```

```python
import functools
import math
import jax
import jax.numpy as jnp
import ml_dtypes
import numpy as np
from jax import lax
from jax.experimental import pallas as pl
from jax.experimental.pallas import tpu as pltpu
from jax.sharding import PartitionSpec as P

OUTER = 24
INNER = 512
HALF = 256


def real_dft(xs):
    n = len(xs)
    if n == 3:
        a, b, c = xs
        t = b + c
        return [(a + t, None), (a - 0.5 * t, (c - b) * math.sin(math.pi / 3))]
    even, odd = (real_dft(xs[0::2]), real_dft(xs[1::2]))
    half = n // 2
    out = [None] * (half + 1)
    out[0] = (even[0][0] + odd[0][0], None)
    out[half] = (even[0][0] - odd[0][0], None)
    for k in range(1, (half + 1) // 2):
        (er, ei), (pr, pi) = (even[k], odd[k])
        c, s = (math.cos(2 * math.pi * k / n), math.sin(2 * math.pi * k / n))
        tr, ti = (pr * c + pi * s, pi * c - pr * s)
        out[k] = (er + tr, ei + ti)
        out[half - k] = (er - tr, ti - ei)
    if half % 2 == 0:
        out[half // 2] = (even[half // 2][0], -odd[half // 2][0])
    return out


def real_dft_back(zs, n):
    if n == 3:
        (c, _), (e, o) = zs
        t, u = (c - 0.5 * e, o * math.sin(math.pi / 3))
        return [c + e, t - u, t + u]
    half = n // 2
    quarter = half // 2
    even = [(zs[0][0] + zs[half][0], None)]
    odd = [(zs[0][0] - zs[half][0], None)]
    for k in range(1, (half + 1) // 2):
        (er, ei), (pr, pi) = (zs[k], zs[half - k])
        even.append((er + pr, ei - pi))
        dr, di = (er - pr, ei + pi)
        c, s = (math.cos(2 * math.pi * k / n), math.sin(2 * math.pi * k / n))
        odd.append((dr * c - di * s, dr * s + di * c))
    if half % 2 == 0:
        even.append((zs[quarter][0], None))
        odd.append((-zs[quarter][1], None))
    first, second = (real_dft_back(even, half), real_dft_back(odd, half))
    return [v for pair in zip(first, second) for v in pair]


def make_tables():
    length = OUTER * INNER
    b = np.arange(INNER)
    q = np.arange(HALF)
    angle = 2 * np.pi * ((b[:, None] * q[None, :]) % INNER) / INNER
    c, s = (np.cos(angle), np.sin(angle))
    table = np.block([[c, -s], [s, c]])
    high = table.astype(ml_dtypes.bfloat16)
    low = (table - high.astype(np.float64)).astype(ml_dtypes.bfloat16)
    twist = 2 * np.pi * ((np.arange(OUTER)[:, None] * b[None, :]) % length) / length
    scale = 2.0 / length
    turns = np.stack(
        [np.cos(twist), np.sin(twist), scale * np.cos(twist), scale * np.sin(twist)]
    ).astype(np.float32)
    weights = np.ones((OUTER, HALF), np.float32)
    weights[0, 0] = 0.5
    return high, low, turns, weights


def split(x):
    high = x.astype(jnp.bfloat16)
    return high, (x - high.astype(jnp.float32)).astype(jnp.bfloat16)


def spectral_chunk(inb, outb, invb, table_hi, table_lo, turns, weights, wide, high, low, narrow, invf):
    levels = 2
    rows = 8

    def widen(k, _):
        invf[k] = invb[k // rows, k % rows].astype(jnp.float32) * weights[...]
        return 0

    lax.fori_loop(0, rows * rows, widen, 0)

    def stage_in(t, _):
        level, tile = (t // 4, t % 4)
        lane = pl.multiple_of(tile * 128, 128)
        xs = [inb[level, :, pl.ds(a * INNER + lane, 128)] for a in range(OUTER)]
        ys = real_dft(xs)
        for p in range(OUTER):
            m = p if p <= OUTER // 2 else OUTER - p
            re, im = ys[m]
            c = turns[0, pl.ds(p, 1), pl.ds(lane, 128)]
            s = turns[1, pl.ds(p, 1), pl.ds(lane, 128)]
            if im is None:
                tr, ti = (re * c, -(re * s))
            elif p <= OUTER // 2:
                tr, ti = (re * c + im * s, im * c - re * s)
            else:
                tr, ti = (re * c - im * s, -(im * c) - re * s)
            where = pl.ds(level * (rows * OUTER) + p, rows, stride=OUTER)
            wide[tile, where, :] = tr
            wide[tile + 4, where, :] = ti
        return 0

    lax.fori_loop(0, 8, stage_in, 0)

    def split_wide(k, _):
        at = pl.ds(pl.multiple_of(k * 32, 32), 32)
        for j in range(8):
            cols = slice(j * 128, j * 128 + 128)
            high[at, cols], low[at, cols] = split(wide[j, at, :])
        return 0

    lax.fori_loop(0, 12, split_wide, 0)

    def forward(n, _):
        cols = pl.ds(pl.multiple_of(n * 256, 256), 256)
        a = jnp.dot(high[...], table_hi[:, cols], preferred_element_type=jnp.float32)
        a += jnp.dot(low[...], table_hi[:, cols], preferred_element_type=jnp.float32)
        a += jnp.dot(high[...], table_lo[:, cols], preferred_element_type=jnp.float32)
        narrow[:, cols] = a
        return 0

    lax.fori_loop(0, 2, forward, 0)

    def solve(t, _):
        pt, lane = (pl.multiple_of((t // 2) * 8, 8), pl.multiple_of((t % 2) * 128, 128))
        spec = [
            [
                narrow[pl.ds((level * rows + s) * OUTER + pt, 8), pl.ds(part * HALF + lane, 128)]
                for level in range(levels)
                for part in range(2)
            ]
            for s in range(rows)
        ]
        for r in range(rows):
            total = [None] * 4
            for s in range(rows):
                factor = invf[r * rows + s, pl.ds(pt, 8), pl.ds(lane, 128)]
                for i in range(4):
                    term = factor * spec[s][i]
                    total[i] = term if total[i] is None else total[i] + term
            for i in range(4):
                level, part = (i // 2, i % 2)
                wide[part * 2 + t % 2, pl.ds((level * rows + r) * OUTER + pt, 8), :] = total[i]
        return 0

    lax.fori_loop(0, 6, solve, 0)

    def split_solved(k, _):
        at = pl.ds(pl.multiple_of(k * 32, 32), 32)
        for j in range(4):
            cols = slice(j * 128, j * 128 + 128)
            high[at, cols], low[at, cols] = split(wide[j, at, :])
        return 0

    lax.fori_loop(0, 12, split_solved, 0)

    def backward(n, _):
        cols = pl.ds(pl.multiple_of(n * 256, 256), 256)
        dims = (((1,), (1,)), ((), ()))
        hi, lo = (high[:, : 2 * HALF], low[:, : 2 * HALF])
        a = lax.dot_general(hi, table_hi[cols, :], dims, preferred_element_type=jnp.float32)
        a += lax.dot_general(lo, table_hi[cols, :], dims, preferred_element_type=jnp.float32)
        a += lax.dot_general(hi, table_lo[cols, :], dims, preferred_element_type=jnp.float32)
        wide[2 * n] = a[:, :128]
        wide[2 * n + 1] = a[:, 128:]
        return 0

    lax.fori_loop(0, 4, backward, 0)

    def stage_out(t, _):
        level, tile = (t // 4, t % 4)
        lane = pl.multiple_of(tile * 128, 128)

        def turned(p):
            where = pl.ds(level * (rows * OUTER) + p, rows, stride=OUTER)
            re = wide[tile, where, :]
            im = wide[tile + 4, where, :]
            c = turns[2, pl.ds(p, 1), pl.ds(lane, 128)]
            s = turns[3, pl.ds(p, 1), pl.ds(lane, 128)]
            return re * c - im * s, re * s + im * c

        zs = []
        for p in range(OUTER // 2 + 1):
            re, im = turned(p)
            if 0 < p < OUTER // 2:
                other_re, other_im = turned(OUTER - p)
                re, im = (re + other_re, im - other_im)
            zs.append((re, im))
        for a, v in enumerate(real_dft_back(zs, OUTER)):
            outb[level, :, pl.ds(a * INNER + lane, 128)] = v
        return 0

    lax.fori_loop(0, 8, stage_out, 0)


zonal_tau = 0.1
merid_tau = 0.5
zonal_cap = 16.0
quad_coef = 0.25
step_size = 0.01
MESH = pl.DeviceIdType.MESH


def make_geometry(bands, members, rows_each):
    total = bands * members * rows_each
    row = np.arange(total, dtype=np.float64)
    cell = np.sin(np.pi * (row + 0.5) / total)
    low = np.where(row > 0, np.sin(np.pi * row / total), 0.0)
    high = np.where(row + 1 < total, np.sin(np.pi * (row + 1) / total), 0.0)
    zonal = zonal_tau * np.minimum(1.0 / (cell * cell), zonal_cap)
    kinds = np.stack([zonal, merid_tau * high / cell, merid_tau * low / cell], -1)
    kinds = kinds.reshape(bands, members, rows_each, 3).transpose(0, 2, 1, 3)
    table = np.zeros((bands, rows_each, members, 8), np.float32)
    table[..., :3] = kinds
    return table.reshape(bands, rows_each, members * 8)


def exchange_kernel(
    bands, members, chunks,
    state, direction, inverses, table_hi_in, table_lo_in, turns_in, weights_in,
    pre, srow, prow, scol, pcol,
    inb, outb, invb, table_hi, table_lo, turns, weights,
    wide, high, low, narrow, invf, edges, scol_out, pcol_out,
    load_sem, edge_sem, own_in, own_out, own_col, send_in, recv_in, send_out, recv_out,
    send_row, recv_row, send_col, recv_col, send_halo, recv_halo,
):
    levels = state.shape[0]
    local_rows = state.shape[1]
    width = state.shape[2]
    rows = 8
    share = chunks * rows
    la, me = (lax.axis_index("lat"), lax.axis_index("lon"))
    up, down = (lax.rem(la + 1, bands), lax.rem(la + bands - 1, bands))
    east, west = (lax.rem(me + 1, members), lax.rem(me + members - 1, members))

    def peer(k):
        y = lax.rem(me // 4 + k // 4, members // 4)
        x = lax.rem(me // 2 + k // 2, 2)
        core = lax.rem(me + k, 2)
        return y * 4 + x * 2 + core

    def remote(src, dst, send, recv, lat, lon):
        return pltpu.make_async_remote_copy(
            src_ref=src, dst_ref=dst, send_sem=send, recv_sem=recv,
            device_id=(lat, lon), device_id_type=MESH,
        )

    barrier = pltpu.get_barrier_semaphore()
    for k in range(1, members):
        pl.semaphore_signal(barrier, inc=1, device_id=(la, peer(k)), device_id_type=MESH)
    for lat in (up, down):
        pl.semaphore_signal(barrier, inc=1, device_id=(lat, me), device_id_type=MESH)

    edge_copies = [
        pltpu.make_async_copy(state.at[:, :, pl.ds(at, 128)], edges.at[side], edge_sem.at[side])
        for side, at in enumerate((0, width - 128))
    ]
    loads = [
        pltpu.make_async_copy(src, dst, load_sem.at[i])
        for i, (src, dst) in enumerate(
            (
                (table_hi_in, table_hi), (table_lo_in, table_lo), (turns_in, turns),
                (weights_in, weights), (inverses, invb),
            )
        )
    ]
    for copy in edge_copies + loads:
        copy.start()
    pl.semaphore_wait(barrier, members + 1)

    def chunk_of(i):
        return lax.rem(i + chunks - 1, chunks)

    def lines(member, c):
        return pl.ds(pl.multiple_of(member * share + c * rows, rows), rows)

    def columns(member):
        return pl.ds(pl.multiple_of(member * width, width), width)

    def send_inputs(i, _):
        c = chunk_of(i)
        for k in range(1, members):
            p = peer(k)
            remote(
                direction.at[:, lines(p, c), :], inb.at[c, :, :, columns(me)],
                send_in, recv_in.at[c], la, p,
            ).start()
        pltpu.make_async_copy(
            direction.at[:, lines(me, c), :], inb.at[c, :, :, columns(me)], own_in.at[c]
        ).start()
        return 0

    lax.fori_loop(0, chunks, send_inputs, 0)
    state_rows = [
        remote(state.at[:, pl.ds(local_rows - rows, rows), :], srow.at[0], send_row.at[0], recv_row.at[0], up, me),
        remote(state.at[:, pl.ds(0, rows), :], srow.at[1], send_row.at[1], recv_row.at[1], down, me),
    ]
    for copy in state_rows:
        copy.start()

    lane = lax.broadcasted_iota(jnp.int32, (rows, 128), 1)
    for copy in edge_copies:
        copy.wait()
    scol_out[...] = jnp.zeros_like(scol_out)

    def pack_state(t, _):
        at = (t // chunks) * 8 + lax.rem(t, chunks)
        for side, first in enumerate((0, 127)):
            for level in range(levels):
                value = edges[side, level, pl.ds(pl.multiple_of(t * rows, rows), rows), :]
                value = pltpu.roll(value, lax.rem(at + 128 - first, 128), 1)
                line = pl.ds(level * rows, rows)
                scol_out[side, line, :] = jnp.where(lane == at, value, scol_out[side, line, :])
        return 0

    lax.fori_loop(0, members * chunks, pack_state, 0)
    pcol_out[...] = jnp.zeros_like(pcol_out)
    state_cols = [
        remote(scol_out.at[1], scol.at[0], send_col.at[0], recv_col.at[0], la, east),
        remote(scol_out.at[0], scol.at[1], send_col.at[1], recv_col.at[1], la, west),
    ]
    for copy in state_cols:
        copy.start()
    for copy in loads:
        copy.wait()

    def arrived(c, sem):
        part = inb.at[c, :, :, pl.ds(0, (members - 1) * width)]
        pltpu.make_async_copy(part, part, sem.at[c]).wait()

    def chunk(i, _):
        c = chunk_of(i)
        arrived(c, recv_in)
        pltpu.make_async_copy(
            direction.at[:, lines(me, c), :], inb.at[c, :, :, columns(me)], own_in.at[c]
        ).wait()
        spectral_chunk(
            inb.at[c], outb.at[c], invb.at[c], table_hi, table_lo, turns, weights,
            wide, high, low, narrow, invf,
        )
        for k in range(1, members):
            p = peer(k)
            remote(
                outb.at[c, :, :, columns(p)], pre.at[:, lines(me, c), :],
                send_out, recv_out.at[c], la, p,
            ).start()
        pltpu.make_async_copy(
            outb.at[c, :, :, columns(me)], pre.at[:, lines(me, c), :], own_out.at[c]
        ).start()

        def pack(d, _):
            tile = width // 128
            before = lax.rem(d * tile + members * tile - 1, members * tile)
            after = lax.rem(d * tile + tile, members * tile)
            held = pcol_out[d]
            for level in range(levels):
                for side, (source, first) in enumerate(((before, 127), (after, 0))):
                    at = c * 4 + level * 2 + side
                    value = outb[c, level, :, pl.ds(pl.multiple_of(source * 128, 128), 128)]
                    value = pltpu.roll(value, lax.rem(at + 128 - first, 128), 1)
                    held = jnp.where(lane == at, value, held)
            pcol_out[d] = held
            return 0

        lax.fori_loop(0, members, pack, 0)
        return 0

    lax.fori_loop(0, chunks, chunk, 0)

    for k in range(1, members):
        p = peer(k)
        remote(pcol_out.at[p], pcol.at[me], send_halo, recv_halo, la, p).start()
    own_halo = pltpu.make_async_copy(pcol_out.at[me], pcol.at[me], own_col)
    own_halo.start()

    def landed(c):
        arrived(c, recv_out)
        pltpu.make_async_copy(
            outb.at[c, :, :, columns(me)], pre.at[:, lines(me, c), :], own_out.at[c]
        ).wait()

    landed(chunks - 1)
    first = remote(pre.at[:, pl.ds(local_rows - rows, rows), :], prow.at[0], send_row.at[2], recv_row.at[2], up, me)
    first.start()
    landed(0)
    second = remote(pre.at[:, pl.ds(0, rows), :], prow.at[1], send_row.at[3], recv_row.at[3], down, me)
    second.start()
    for c in range(1, chunks - 1):
        landed(c)
    others = pcol_out.at[pl.ds(0, members - 1)]
    pltpu.make_async_copy(others, others, recv_halo).wait()
    pltpu.make_async_copy(others, others, send_halo).wait()
    own_halo.wait()
    for copy in state_rows + state_cols + [first, second]:
        copy.wait()
    everything = inb.at[:, :, :, pl.ds(0, (members - 1) * width)]
    pltpu.make_async_copy(everything, everything, send_in).wait()
    pltpu.make_async_copy(everything, everything, send_out).wait()


def exchange(state, direction, inverses, bands, members):
    levels, local_rows, width = state.shape
    chunks = inverses.shape[0]
    high, low, turns, weights = make_tables()
    f32 = jnp.float32
    anywhere = pl.BlockSpec(memory_space=pl.ANY)
    dma = pltpu.SemaphoreType.DMA
    return pl.pallas_call(
        functools.partial(exchange_kernel, bands, members, chunks),
        out_shape=(
            jax.ShapeDtypeStruct(state.shape, f32),
            jax.ShapeDtypeStruct((2, levels, 8, width), f32),
            jax.ShapeDtypeStruct((2, levels, 8, width), f32),
            jax.ShapeDtypeStruct((2, levels * 8, 128), f32),
            jax.ShapeDtypeStruct((members, 8, 128), f32),
        ),
        in_specs=[anywhere] * 7,
        out_specs=(anywhere,) * 5,
        scratch_shapes=[
            pltpu.VMEM((chunks, levels, 8, members * width), f32),
            pltpu.VMEM((chunks, levels, 8, members * width), f32),
            pltpu.VMEM(inverses.shape, jnp.bfloat16),
            pltpu.VMEM(high.shape, jnp.bfloat16),
            pltpu.VMEM(low.shape, jnp.bfloat16),
            pltpu.VMEM(turns.shape, f32),
            pltpu.VMEM(weights.shape, f32),
            pltpu.VMEM((8, levels * 8 * OUTER, 128), f32),
            pltpu.VMEM((levels * 8 * OUTER, 2 * INNER), jnp.bfloat16),
            pltpu.VMEM((levels * 8 * OUTER, 2 * INNER), jnp.bfloat16),
            pltpu.VMEM((levels * 8 * OUTER, INNER), f32),
            pltpu.VMEM((64, OUTER, HALF), f32),
            pltpu.VMEM((2, levels, local_rows, 128), f32),
            pltpu.VMEM((2, levels * 8, 128), f32),
            pltpu.VMEM((members, 8, 128), f32),
            dma((5,)), dma((2,)), dma((chunks,)), dma((chunks,)), dma,
            dma, dma((chunks,)), dma, dma((chunks,)),
            dma((4,)), dma((4,)), dma((2,)), dma((2,)), dma, dma,
        ],
        compiler_params=pltpu.CompilerParams(
            collective_id=0, has_side_effects=True, vmem_limit_bytes=60 << 20
        ),
        name="exchange",
    )(state, direction, inverses, jnp.asarray(high), jnp.asarray(low), jnp.asarray(turns), jnp.asarray(weights))


def face(a, b, pa, pb):
    s, p, d, dp = (a + b, pa + pb, b - a, pb - pa)
    moved = s + step_size * p
    return dp + (0.25 * quad_coef) * (moved * moved * dp + p * (s + moved) * d)


def stencil_kernel(
    members, chunks,
    state, before_s, after_s, pre, before_p, after_p, kappa, srow, prow, scol, pcol, geometry,
    pre_out, jac_out,
):
    j = pl.program_id(0)
    levels, _, width = state.shape
    rows = 8
    turn = lax.rem(128 - 8 * j, 128)
    geo = pltpu.roll(geometry[...], turn, 1)
    row = lax.broadcasted_iota(jnp.int32, (rows, width), 0)
    lane = lax.broadcasted_iota(jnp.int32, (rows, width), 1)
    for level in range(levels):
        west_s = pltpu.roll(scol[0, level * rows : level * rows + rows, :], turn, 1)
        east_s = pltpu.roll(scol[1, level * rows : level * rows + rows, :], turn, 1)
        tiles_s = [jnp.where(j == 0, srow[0, level], before_s[level])]
        tiles_p = [jnp.where(j == 0, prow[0, level], before_p[level])]
        for c in range(chunks):
            tiles_s.append(state[level, c * rows : c * rows + rows, :])
            tiles_p.append(pre[level, c * rows : c * rows + rows, :])
        last = j == members - 1
        tiles_s.append(jnp.where(last, srow[1, level], after_s[level]))
        tiles_p.append(jnp.where(last, prow[1, level], after_p[level]))

        def ahead(tiles, c):
            return jnp.where(row == rows - 1, pltpu.roll(tiles[c + 1], rows - 1, 0), pltpu.roll(tiles[c], rows - 1, 0))

        def north_face(c):
            return face(tiles_s[c], ahead(tiles_s, c), tiles_p[c], ahead(tiles_p, c))

        below = pltpu.roll(north_face(0), 1, 0)
        for c in range(chunks):
            w, p = (tiles_s[c + 1], tiles_p[c + 1])
            at = c * 4 + level * 2
            line = slice(c * rows, c * rows + rows)
            w_east = jnp.where(lane == width - 1, east_s[:, c : c + 1], pltpu.roll(w, width - 1, 1))
            p_east = jnp.where(lane == width - 1, pcol[0, :, at + 1 : at + 2], pltpu.roll(p, width - 1, 1))
            east = face(w, w_east, p, p_east)
            edge = face(west_s[:, c : c + 1], w[:, :1], pcol[0, :, at : at + 1], p[:, :1])
            west = jnp.where(lane == 0, edge, pltpu.roll(east, 1, 1))
            north = north_face(c + 1)
            turned = pltpu.roll(north, 1, 0)
            south = jnp.where(row == 0, below, turned)
            below = turned
            spread = geo[line, 0:1] * (east - west) + (geo[line, 1:2] * north - geo[line, 2:3] * south)
            pre_out[level, line, :] = p
            jac_out[level, line, :] = p - kappa[line, :].astype(jnp.float32) * spread


def stencil(state, pre, diffusivity, srow, prow, scol, pcol, geometry, members):
    levels, local_rows, width = state.shape
    share = local_rows // members
    chunks = share // 8
    final = local_rows // 8 - 1
    block = pl.BlockSpec((levels, share, width), lambda j: (0, j, 0))
    before = pl.BlockSpec((levels, 8, width), lambda j: (0, jnp.maximum(j * chunks - 1, 0), 0))
    after = pl.BlockSpec((levels, 8, width), lambda j: (0, jnp.minimum(j * chunks + chunks, final), 0))

    def whole(x):
        return pl.BlockSpec(x.shape, lambda j: (0,) * x.ndim)

    return pl.pallas_call(
        functools.partial(stencil_kernel, members, chunks),
        grid=(members,),
        out_shape=(jax.ShapeDtypeStruct(state.shape, jnp.float32),) * 2,
        in_specs=[
            block, before, after, block, before, after,
            pl.BlockSpec((share, width), lambda j: (j, 0)),
            whole(srow), whole(prow), whole(scol),
            pl.BlockSpec((1, 8, 128), lambda j: (j, 0, 0)),
            whole(geometry),
        ],
        out_specs=(block, block),
        compiler_params=pltpu.CompilerParams(vmem_limit_bytes=48 << 20),
        name="stencil",
    )(state, state, state, pre, pre, pre, diffusivity, srow, prow, scol, pcol, geometry)


def on_device(bands, members, state, direction, diffusivity, inverses):
    local_rows = state.shape[1]
    pre, srow, prow, scol, pcol = exchange(state, direction, inverses, bands, members)
    table = jnp.asarray(make_geometry(bands, members, local_rows // members))
    geometry = lax.dynamic_index_in_dim(table, lax.axis_index("lat"), 0, keepdims=False)
    return stencil(state, pre, diffusivity, srow, prow, scol, pcol, geometry, members)


def solution(mesh):
    return jax.shard_map(
        functools.partial(on_device, mesh.shape["lat"], mesh.shape["lon"]),
        mesh=mesh,
        in_specs=(
            P(None, "lat", "lon"),
            P(None, "lat", "lon"),
            P("lat", "lon"),
            P(("lat", "lon"), None, None, None, None),
        ),
        out_specs=(P(None, "lat", "lon"), P(None, "lat", "lon")),
        check_vma=False,
    )
```

```python
import functools
import math
import jax
import jax.numpy as jnp
import ml_dtypes
import numpy as np
from jax import lax
from jax.experimental import pallas as pl
from jax.experimental.pallas import tpu as pltpu
from jax.sharding import PartitionSpec as P

OUTER = 24
INNER = 512
HALF = 256


def real_dft(xs):
    n = len(xs)
    if n == 3:
        a, b, c = xs
        t = b + c
        return [(a + t, None), (a - 0.5 * t, (c - b) * math.sin(math.pi / 3))]
    even, odd = (real_dft(xs[0::2]), real_dft(xs[1::2]))
    half = n // 2
    out = [None] * (half + 1)
    out[0] = (even[0][0] + odd[0][0], None)
    out[half] = (even[0][0] - odd[0][0], None)
    for k in range(1, (half + 1) // 2):
        (er, ei), (pr, pi) = (even[k], odd[k])
        c, s = (math.cos(2 * math.pi * k / n), math.sin(2 * math.pi * k / n))
        tr, ti = (pr * c + pi * s, pi * c - pr * s)
        out[k] = (er + tr, ei + ti)
        out[half - k] = (er - tr, ti - ei)
    if half % 2 == 0:
        out[half // 2] = (even[half // 2][0], -odd[half // 2][0])
    return out


def real_dft_back(zs, n):
    if n == 3:
        (c, _), (e, o) = zs
        t, u = (c - 0.5 * e, o * math.sin(math.pi / 3))
        return [c + e, t - u, t + u]
    half = n // 2
    quarter = half // 2
    even = [(zs[0][0] + zs[half][0], None)]
    odd = [(zs[0][0] - zs[half][0], None)]
    for k in range(1, (half + 1) // 2):
        (er, ei), (pr, pi) = (zs[k], zs[half - k])
        even.append((er + pr, ei - pi))
        dr, di = (er - pr, ei + pi)
        c, s = (math.cos(2 * math.pi * k / n), math.sin(2 * math.pi * k / n))
        odd.append((dr * c - di * s, dr * s + di * c))
    if half % 2 == 0:
        even.append((zs[quarter][0], None))
        odd.append((-zs[quarter][1], None))
    first, second = (real_dft_back(even, half), real_dft_back(odd, half))
    return [v for pair in zip(first, second) for v in pair]


def make_tables():
    length = OUTER * INNER
    b = np.arange(INNER)
    q = np.arange(HALF)
    angle = 2 * np.pi * ((b[:, None] * q[None, :]) % INNER) / INNER
    c, s = (np.cos(angle), np.sin(angle))
    table = np.block([[c, -s], [s, c]])
    high = table.astype(ml_dtypes.bfloat16)
    low = (table - high.astype(np.float64)).astype(ml_dtypes.bfloat16)
    twist = 2 * np.pi * ((np.arange(OUTER)[:, None] * b[None, :]) % length) / length
    scale = 2.0 / length
    turns = np.stack(
        [np.cos(twist), np.sin(twist), scale * np.cos(twist), scale * np.sin(twist)]
    ).astype(np.float32)
    weights = np.ones((OUTER, HALF), np.float32)
    weights[0, 0] = 0.5
    return high, low, turns, weights


def split(x):
    high = x.astype(jnp.bfloat16)
    return high, (x - high.astype(jnp.float32)).astype(jnp.bfloat16)


def spectral_chunk(inb, outb, invb, table_hi, table_lo, turns, weights, wide, high, low, narrow, invf):
    levels = 2
    rows = 8

    def widen(k, _):
        invf[k] = invb[k // rows, k % rows].astype(jnp.float32) * weights[...]
        return 0

    lax.fori_loop(0, rows * rows, widen, 0)

    def stage_in(t, _):
        level, tile = (t // 4, t % 4)
        lane = pl.multiple_of(tile * 128, 128)
        xs = [inb[level, :, pl.ds(a * INNER + lane, 128)] for a in range(OUTER)]
        ys = real_dft(xs)
        for p in range(OUTER):
            m = p if p <= OUTER // 2 else OUTER - p
            re, im = ys[m]
            c = turns[0, pl.ds(p, 1), pl.ds(lane, 128)]
            s = turns[1, pl.ds(p, 1), pl.ds(lane, 128)]
            if im is None:
                tr, ti = (re * c, -(re * s))
            elif p <= OUTER // 2:
                tr, ti = (re * c + im * s, im * c - re * s)
            else:
                tr, ti = (re * c - im * s, -(im * c) - re * s)
            where = pl.ds(level * (rows * OUTER) + p, rows, stride=OUTER)
            wide[tile, where, :] = tr
            wide[tile + 4, where, :] = ti
        return 0

    lax.fori_loop(0, 8, stage_in, 0)

    def split_wide(k, _):
        at = pl.ds(pl.multiple_of(k * 32, 32), 32)
        for j in range(8):
            cols = slice(j * 128, j * 128 + 128)
            high[at, cols], low[at, cols] = split(wide[j, at, :])
        return 0

    lax.fori_loop(0, 12, split_wide, 0)

    def forward(n, _):
        cols = pl.ds(pl.multiple_of(n * 256, 256), 256)
        a = jnp.dot(high[...], table_hi[:, cols], preferred_element_type=jnp.float32)
        a += jnp.dot(low[...], table_hi[:, cols], preferred_element_type=jnp.float32)
        a += jnp.dot(high[...], table_lo[:, cols], preferred_element_type=jnp.float32)
        narrow[:, cols] = a
        return 0

    lax.fori_loop(0, 2, forward, 0)

    def solve(t, _):
        pt, lane = (pl.multiple_of((t // 2) * 8, 8), pl.multiple_of((t % 2) * 128, 128))
        spec = [
            [
                narrow[pl.ds((level * rows + s) * OUTER + pt, 8), pl.ds(part * HALF + lane, 128)]
                for level in range(levels)
                for part in range(2)
            ]
            for s in range(rows)
        ]
        for r in range(rows):
            total = [None] * 4
            for s in range(rows):
                factor = invf[r * rows + s, pl.ds(pt, 8), pl.ds(lane, 128)]
                for i in range(4):
                    term = factor * spec[s][i]
                    total[i] = term if total[i] is None else total[i] + term
            for i in range(4):
                level, part = (i // 2, i % 2)
                wide[part * 2 + t % 2, pl.ds((level * rows + r) * OUTER + pt, 8), :] = total[i]
        return 0

    lax.fori_loop(0, 6, solve, 0)

    def split_solved(k, _):
        at = pl.ds(pl.multiple_of(k * 32, 32), 32)
        for j in range(4):
            cols = slice(j * 128, j * 128 + 128)
            high[at, cols], low[at, cols] = split(wide[j, at, :])
        return 0

    lax.fori_loop(0, 12, split_solved, 0)

    def backward(n, _):
        cols = pl.ds(pl.multiple_of(n * 256, 256), 256)
        dims = (((1,), (1,)), ((), ()))
        hi, lo = (high[:, : 2 * HALF], low[:, : 2 * HALF])
        a = lax.dot_general(hi, table_hi[cols, :], dims, preferred_element_type=jnp.float32)
        a += lax.dot_general(lo, table_hi[cols, :], dims, preferred_element_type=jnp.float32)
        a += lax.dot_general(hi, table_lo[cols, :], dims, preferred_element_type=jnp.float32)
        wide[2 * n] = a[:, :128]
        wide[2 * n + 1] = a[:, 128:]
        return 0

    lax.fori_loop(0, 4, backward, 0)

    def stage_out(t, _):
        level, tile = (t // 4, t % 4)
        lane = pl.multiple_of(tile * 128, 128)

        def turned(p):
            where = pl.ds(level * (rows * OUTER) + p, rows, stride=OUTER)
            re = wide[tile, where, :]
            im = wide[tile + 4, where, :]
            c = turns[2, pl.ds(p, 1), pl.ds(lane, 128)]
            s = turns[3, pl.ds(p, 1), pl.ds(lane, 128)]
            return re * c - im * s, re * s + im * c

        zs = []
        for p in range(OUTER // 2 + 1):
            re, im = turned(p)
            if 0 < p < OUTER // 2:
                other_re, other_im = turned(OUTER - p)
                re, im = (re + other_re, im - other_im)
            zs.append((re, im))
        for a, v in enumerate(real_dft_back(zs, OUTER)):
            outb[level, a * (INNER // 128) + tile] = v
        return 0

    lax.fori_loop(0, 8, stage_out, 0)


zonal_tau = 0.1
merid_tau = 0.5
zonal_cap = 16.0
quad_coef = 0.25
step_size = 0.01
LIMIT = 36
MESH = pl.DeviceIdType.MESH


def make_geometry(bands, members, rows_each):
    total = bands * members * rows_each
    row = np.arange(total, dtype=np.float64)
    cell = np.sin(np.pi * (row + 0.5) / total)
    low = np.where(row > 0, np.sin(np.pi * row / total), 0.0)
    high = np.where(row + 1 < total, np.sin(np.pi * (row + 1) / total), 0.0)
    zonal = zonal_tau * np.minimum(1.0 / (cell * cell), zonal_cap)
    kinds = np.stack([zonal, merid_tau * high / cell, merid_tau * low / cell], -1)
    kinds = (0.25 * quad_coef) * kinds.reshape(bands, members, rows_each, 3)
    table = np.zeros((bands, rows_each + members, members, 8), np.float32)
    table[:, :rows_each, :, :3] = kinds.transpose(0, 2, 1, 3)
    table = table.reshape(bands, rows_each + members, members * 8)
    table[:, rows_each:, 0] = kinds[:, :, rows_each - 17, 1]
    table[:, rows_each:, 1] = kinds[:, :, rows_each - 8, 2]
    return table


def face(a, b, pa, pb):
    s, p, d, dp = (a + b, pa + pb, b - a, pb - pa)
    moved = s + step_size * p
    return (4.0 / quad_coef + moved * moved) * dp + p * (s + moved) * d


def stencil_tile(j, c, chunks, field, pre, kappa, scol, pcol, geometry, jac, skip="", target=None):
    levels, tiles = field.shape[:2]
    rows = 8
    line = pl.multiple_of((j * chunks + c) * rows, rows)
    base = line + rows
    own = pl.ds(pl.multiple_of(c * rows, rows), rows)
    target = line if target is None else pl.multiple_of(target, rows)
    lane = lax.broadcasted_iota(jnp.int32, (rows, 128), 1)
    first, last = (lane == 0, lane == 127)
    row = lax.broadcasted_iota(jnp.int32, (rows, 128), 0)
    geo = pltpu.roll(geometry[own, :], lax.rem(128 - 8 * j, 128), 1)
    zonal, above, below = [jnp.broadcast_to(geo[:, i : i + 1], (rows, 128)) for i in range(3)]

    def to_end(tile, at):
        return pltpu.roll(tile, lax.rem(255 - at, 128), 1)

    for level in range(levels):
        side = slice(level * rows, level * rows + rows)
        w = [field[level, k, pl.ds(base, rows), :] for k in range(tiles)]
        p = [pre[level, k, pl.ds(base, rows), :] for k in range(tiles)]
        rw = [pltpu.roll(x, 127, 1) for x in w] + [to_end(scol[1, side, :], 8 * j + c)]
        rp = [pltpu.roll(x, 127, 1) for x in p] + [to_end(pcol[j], 4 * c + 2 * level + 1)]
        edge = face(
            to_end(scol[0, side, :], 8 * j + c), rw[0], to_end(pcol[j], 4 * c + 2 * level), rp[0]
        )
        behind = pltpu.roll(edge, 1, 1)
        for k in range(tiles):
            east = face(
                w[k], jnp.where(last, rw[k + 1], rw[k]), p[k], jnp.where(last, rp[k + 1], rp[k])
            )
            turned = pltpu.roll(east, 1, 1)
            west = jnp.where(first, behind, turned)
            behind = turned
            if skip == "north":
                p_north = pltpu.roll(p[k], rows - 1, 0)
            else:
                p_north = pre[level, k, pl.ds(base + 1, rows), :]
            if skip == "south":
                p_south = pltpu.roll(p[k], 1, 0)
            else:
                p_south = pre[level, k, pl.ds(base - 1, rows), :]
            north = above * face(w[k], field[level, k, pl.ds(base + 1, rows), :], p[k], p_north)
            south = below * face(field[level, k, pl.ds(base - 1, rows), :], w[k], p_south, p[k])
            if skip == "north":
                north = jnp.where(row == rows - 1, 0.0, north)
            if skip == "south":
                south = jnp.where(row == 0, 0.0, south)
            spread = zonal * (east - west) + (north - south)
            jac[level, k, pl.ds(target, rows), :] = p[k] - kappa[k, pl.ds(line, rows), :] * spread


def exchange_kernel(
    bands, members, chunks,
    state, direction, diffusivity, inverses, table_hi_in, table_lo_in, turns_in, weights_in, geometry_in,
    field, pre, jac, kappa, scol, pcol,
    inb, outb, invb, table_hi, table_lo, turns, weights, geometry, kappa_in,
    wide, high, low, narrow, invf, scol_out, pcol_out, row_out, row_in,
    load_sem, field_sem, own_in, own_out, own_col, send_in, recv_in, send_out, recv_out,
    send_row, recv_row, send_col, recv_col, send_halo, recv_halo,
):
    levels, local_rows, width = state.shape
    rows = 8
    tiles = width // 128
    share = chunks * rows
    la, me = (lax.axis_index("lat"), lax.axis_index("lon"))
    up, down = (lax.rem(la + 1, bands), lax.rem(la + bands - 1, bands))
    east, west = (lax.rem(me + 1, members), lax.rem(me + members - 1, members))

    def peer(k):
        y = lax.rem(me // 4 + k // 4, members // 4)
        x = lax.rem(me // 2 + k // 2, 2)
        core = lax.rem(me + k, 2)
        return y * 4 + x * 2 + core

    def remote(src, dst, send, recv, lat, lon):
        return pltpu.make_async_remote_copy(
            src_ref=src, dst_ref=dst, send_sem=send, recv_sem=recv,
            device_id=(lat, lon), device_id_type=MESH,
        )

    barrier = pltpu.get_barrier_semaphore()
    for k in range(1, members):
        pl.semaphore_signal(barrier, inc=1, device_id=(la, peer(k)), device_id_type=MESH)
    for lat in (up, down):
        pl.semaphore_signal(barrier, inc=1, device_id=(lat, me), device_id_type=MESH)

    field_copies = [
        pltpu.make_async_copy(
            state.at[:, :, pl.ds(k * 128, 128)], field.at[:, k, pl.ds(rows, local_rows), :], field_sem.at[k]
        )
        for k in range(tiles)
    ]
    kappa_copies = [
        pltpu.make_async_copy(diffusivity.at[:, pl.ds(k * 128, 128)], kappa_in.at[k], field_sem.at[tiles + k])
        for k in range(tiles)
    ]
    loads = [
        pltpu.make_async_copy(src, dst, load_sem.at[i])
        for i, (src, dst) in enumerate(
            (
                (table_hi_in, table_hi), (table_lo_in, table_lo), (turns_in, turns),
                (weights_in, weights), (inverses, invb), (geometry_in.at[la], geometry),
            )
        )
    ]
    for copy in field_copies + loads + kappa_copies:
        copy.start()
    pl.semaphore_wait(barrier, members + 1)

    def chunk_of(i):
        return lax.rem(i + chunks - 1, chunks)

    def lines(member, c):
        return pl.ds(pl.multiple_of(member * share + c * rows, rows), rows)

    def landing(member, c):
        return pl.ds(pl.multiple_of(member * share + c * rows + rows, rows), rows)

    def columns(member):
        return pl.ds(pl.multiple_of(member * width, width), width)

    def send_inputs(i, _):
        c = chunk_of(i)
        for k in range(1, members):
            p = peer(k)
            remote(
                direction.at[:, lines(p, c), :], inb.at[c, :, :, columns(me)],
                send_in, recv_in.at[c], la, p,
            ).start()
        pltpu.make_async_copy(
            direction.at[:, lines(me, c), :], inb.at[c, :, :, columns(me)], own_in.at[c]
        ).start()
        return 0

    lax.fori_loop(0, chunks, send_inputs, 0)

    lane = lax.broadcasted_iota(jnp.int32, (rows, 128), 1)
    for copy in field_copies:
        copy.wait()
    scol_out[...] = jnp.zeros_like(scol_out)

    def pack_state(t, _):
        at = (t // chunks) * 8 + lax.rem(t, chunks)
        for side, (k, spot) in enumerate(((0, 0), (tiles - 1, 127))):
            for level in range(levels):
                value = field[level, k, pl.ds(pl.multiple_of(t * rows + rows, rows), rows), :]
                value = pltpu.roll(value, lax.rem(at + 128 - spot, 128), 1)
                line = pl.ds(level * rows, rows)
                scol_out[side, line, :] = jnp.where(lane == at, value, scol_out[side, line, :])
        return 0

    lax.fori_loop(0, members * chunks, pack_state, 0)
    row_out[...] = jnp.zeros_like(row_out)

    def pack_row(source, line, slot):
        for level in range(levels):
            for k in range(tiles):
                at = level * tiles + k
                row_out[slot, at : at + 1, :] = source[level, k, line : line + 1, :]

    def unpack_row(target, line, slot):
        for level in range(levels):
            for k in range(tiles):
                at = level * tiles + k
                target[level, k, line : line + 1, :] = row_in[slot, at : at + 1, :]

    def row_copy(slot, lat):
        return remote(row_out.at[slot], row_in.at[slot], send_row.at[slot], recv_row.at[slot], lat, me)

    top, bottom = (rows + local_rows - 1, rows)
    pack_row(field, top, 0)
    pack_row(field, bottom, 1)
    pcol_out[...] = jnp.zeros_like(pcol_out)
    small = [
        remote(scol_out.at[1], scol.at[0], send_col.at[0], recv_col.at[0], la, east),
        remote(scol_out.at[0], scol.at[1], send_col.at[1], recv_col.at[1], la, west),
        row_copy(0, up),
        row_copy(1, down),
    ]
    for copy in small:
        copy.start()
    for copy in kappa_copies:
        copy.wait()

    def widen_kappa(t, _):
        at = pl.ds(pl.multiple_of(t * 32, 32), 32)
        for k in range(tiles):
            kappa[k, at, :] = kappa_in[k, at, :].astype(jnp.float32)
        return 0

    lax.fori_loop(0, local_rows // 32, widen_kappa, 0)
    for copy in loads:
        copy.wait()

    def chunk(i, _):
        c = chunk_of(i)
        part = inb.at[c, :, :, pl.ds(0, (members - 1) * width)]
        pltpu.make_async_copy(part, part, recv_in.at[c]).wait()
        pltpu.make_async_copy(
            direction.at[:, lines(me, c), :], inb.at[c, :, :, columns(me)], own_in.at[c]
        ).wait()
        spectral_chunk(
            inb.at[c], outb.at[c], invb.at[c], table_hi, table_lo, turns, weights,
            wide, high, low, narrow, invf,
        )

        slot = i // (chunks - 1)

        def pack(d, _):
            before = lax.rem(d * tiles + members * tiles - 1, members * tiles)
            after = lax.rem(d * tiles + tiles, members * tiles)
            held = pcol_out[slot, d]
            for level in range(levels):
                for side, (source, spot) in enumerate(((before, 127), (after, 0))):
                    at = c * 4 + level * 2 + side
                    value = pltpu.roll(outb[c, level, source], lax.rem(at + 128 - spot, 128), 1)
                    held = jnp.where(lane == at, value, held)
            pcol_out[slot, d] = held
            return 0

        lax.fori_loop(0, members, pack, 0)

        @pl.when(i >= chunks - 2)
        def _():
            for k in range(1, members):
                p = peer(k)
                remote(
                    pcol_out.at[slot, p], pcol.at[slot, me], send_halo.at[slot], recv_halo.at[slot], la, p
                ).start()
            pltpu.make_async_copy(pcol_out.at[slot, me], pcol.at[slot, me], own_col.at[slot]).start()

        for k in range(1, members):
            p = peer(k)
            remote(
                outb.at[c, :, pl.ds(p * tiles, tiles)], pre.at[:, :, landing(me, c), :],
                send_out, recv_out.at[c], la, p,
            ).start()
        pltpu.make_async_copy(
            outb.at[c, :, pl.ds(me * tiles, tiles)], pre.at[:, :, landing(me, c), :], own_out.at[c]
        ).start()
        return 0

    lax.fori_loop(0, chunks, chunk, 0)

    def landed(c):
        part = outb.at[c, :, pl.ds(0, (members - 1) * tiles)]
        pltpu.make_async_copy(part, part, recv_out.at[c]).wait()
        pltpu.make_async_copy(
            outb.at[c, :, pl.ds(me * tiles, tiles)], pre.at[:, :, landing(me, c), :], own_out.at[c]
        ).wait()

    def stencil(c, low, high, skip=""):
        def one(j, _):
            stencil_tile(j, c, chunks, field, pre, kappa, scol, pcol.at[0], geometry, jac, skip)
            return 0

        lax.fori_loop(low, high, one, 0)

    def halo(slot):
        others = pcol_out.at[slot, pl.ds(0, members - 1)]
        pltpu.make_async_copy(others, others, recv_halo.at[slot]).wait()
        pltpu.make_async_copy(pcol_out.at[slot, me], pcol.at[slot, me], own_col.at[slot]).wait()
        pltpu.make_async_copy(others, others, send_halo.at[slot]).wait()

    final = chunks - 1
    for copy in small:
        copy.wait()
    unpack_row(field, bottom - 1, 0)
    unpack_row(field, top + 1, 1)
    landed(final)
    pack_row(pre, top, 2)
    first = row_copy(2, up)
    first.start()
    landed(0)
    pack_row(pre, bottom, 3)
    second = row_copy(3, down)
    second.start()
    for c in range(1, chunks - 3):
        landed(c)
    halo(0)
    stencil(0, 1, members)
    lax.fori_loop(1, chunks - 4, lambda c, _: (stencil(c, 0, members), 0)[1], 0)
    stencil(final, 0, members - 1, "south")
    landed(chunks - 3)
    stencil(chunks - 4, 0, members)
    stencil(chunks - 3, 0, members, "north")
    first.wait()
    second.wait()
    unpack_row(pre, bottom - 1, 2)
    unpack_row(pre, top + 1, 3)
    stencil(0, 0, 1)
    stencil(final, members - 1, members, "south")
    landed(chunks - 2)
    halo(1)
    part = inb.at[:, :, :, pl.ds(0, (members - 1) * width)]
    pltpu.make_async_copy(part, part, send_in).wait()
    part = outb.at[:, :, pl.ds(0, (members - 1) * tiles)]
    pltpu.make_async_copy(part, part, send_out).wait()


def finish_kernel(
    members, chunks, field, pre, jac, kappa, scol, pcol, geometry_in,
    pre_out, jac_out, work, geometry, geo_sem, pre_sem, early_sem, late_sem,
):
    levels, tiles = field.shape[:2]
    rows = 8
    share = chunks * rows
    late = 3 * rows
    early = share - late
    geo = pltpu.make_async_copy(geometry_in.at[lax.axis_index("lat")], geometry, geo_sem)
    geo.start()
    count = members * share

    def lane_tile(k):
        return pl.ds(k * 128, 128)

    pre_copies = [
        pltpu.make_async_copy(
            pre.at[:, k, pl.ds(rows, count), :], pre_out.at[:, :, lane_tile(k)], pre_sem.at[k]
        )
        for k in range(tiles)
    ]

    def early_copy(j, k):
        line = pl.ds(pl.multiple_of(j * share, rows), early)
        return pltpu.make_async_copy(
            jac.at[:, k, line, :], jac_out.at[:, line, lane_tile(k)], early_sem.at[k, j]
        )

    def late_copy(j, k):
        line = pl.ds(pl.multiple_of(j * share + early, rows), late)
        return pltpu.make_async_copy(
            work.at[:, k, pl.ds(pl.multiple_of(j * late, rows), late), :],
            jac_out.at[:, line, lane_tile(k)], late_sem.at[k, j],
        )

    def start_early(j, _):
        for k in range(tiles):
            early_copy(j, k).start()
        return 0

    geo.wait()
    for copy in pre_copies:
        copy.start()
    lax.fori_loop(0, members, start_early, 0)

    def group(g, _):
        def take(j, _):
            for level in range(levels):
                for k in range(tiles):
                    for at in (0, late - rows):
                        source = pl.ds(pl.multiple_of(j * share + early + at, rows), rows)
                        target = pl.ds(pl.multiple_of(j * late + at, rows), rows)
                        work[level, k, target, :] = jac[level, k, source, :]
            return 0

        lax.fori_loop(g * rows, g * rows + rows, take, 0)
        factor = geometry[pl.ds(pl.multiple_of(share + g * rows, rows), rows), :]
        above, below = [jnp.broadcast_to(factor[:, i : i + 1], (rows, 128)) for i in range(2)]

        def every(at, padded=0):
            return pl.ds(g * rows * share + early + at + padded, rows, stride=share)

        for level in range(levels):
            for k in range(tiles):
                def pair(at):
                    lower, upper = (every(at, rows), every(at + 1, rows))
                    return face(field[level, k, lower, :], field[level, k, upper, :], pre[level, k, lower, :], pre[level, k, upper, :])

                low_at, high_at = (rows - 1, late - rows)
                fixed = jac[level, k, every(low_at), :] - kappa[k, every(low_at), :] * (above * pair(low_at))
                work[level, k, pl.ds(g * rows * late + low_at, rows, stride=late), :] = fixed
                fixed = jac[level, k, every(high_at), :] + kappa[k, every(high_at), :] * (below * pair(high_at - 1))
                work[level, k, pl.ds(g * rows * late + high_at, rows, stride=late), :] = fixed

        def one(j, _):
            stencil_tile(
                j, chunks - 2, chunks, field, pre, kappa, scol, pcol.at[1], geometry,
                work, "", j * late + rows,
            )
            for k in range(tiles):
                late_copy(j, k).start()
            return 0

        lax.fori_loop(g * rows, g * rows + rows, one, 0)
        return 0

    lax.fori_loop(0, members // rows, group, 0)

    def drain(j, _):
        for k in range(tiles):
            early_copy(j, k).wait()
            late_copy(j, k).wait()
        return 0

    lax.fori_loop(0, members, drain, 0)
    for copy in pre_copies:
        copy.wait()


def on_device(bands, members, state, direction, diffusivity, inverses):
    levels, local_rows, width = state.shape
    chunks = inverses.shape[0]
    tiles = width // 128
    share = local_rows // members
    table_hi, table_lo, turns, weights = make_tables()
    geometry = jnp.asarray(make_geometry(bands, members, share))
    f32 = jnp.float32
    anywhere = pl.BlockSpec(memory_space=pl.ANY)
    on_chip = pl.BlockSpec(memory_space=pltpu.VMEM)
    dma = pltpu.SemaphoreType.DMA
    padded = (levels, tiles, local_rows + 16, 128)
    parts = pl.pallas_call(
        functools.partial(exchange_kernel, bands, members, chunks),
        out_shape=(
            pltpu.VMEM(padded, f32),
            pltpu.VMEM(padded, f32),
            pltpu.VMEM((levels, tiles, local_rows, 128), f32),
            pltpu.VMEM((tiles, local_rows, 128), f32),
            pltpu.VMEM((2, levels * 8, 128), f32),
            pltpu.VMEM((2, members, 8, 128), f32),
        ),
        in_specs=[pl.BlockSpec(memory_space=pltpu.HBM)] * 9,
        out_specs=(on_chip,) * 6,
        scratch_shapes=[
            pltpu.VMEM((chunks, levels, 8, members * width), f32),
            pltpu.VMEM((chunks, levels, members * tiles, 8, 128), f32),
            pltpu.VMEM(inverses.shape, jnp.bfloat16),
            pltpu.VMEM(table_hi.shape, jnp.bfloat16),
            pltpu.VMEM(table_lo.shape, jnp.bfloat16),
            pltpu.VMEM(turns.shape, f32),
            pltpu.VMEM(weights.shape, f32),
            pltpu.VMEM(geometry.shape[1:], f32),
            pltpu.VMEM((tiles, local_rows, 128), jnp.bfloat16),
            pltpu.VMEM((8, levels * 8 * OUTER, 128), f32),
            pltpu.VMEM((levels * 8 * OUTER, 2 * INNER), jnp.bfloat16),
            pltpu.VMEM((levels * 8 * OUTER, 2 * INNER), jnp.bfloat16),
            pltpu.VMEM((levels * 8 * OUTER, INNER), f32),
            pltpu.VMEM((64, OUTER, HALF), f32),
            pltpu.VMEM((2, levels * 8, 128), f32),
            pltpu.VMEM((2, members, 8, 128), f32),
            pltpu.VMEM((4, 16, 128), f32),
            pltpu.VMEM((4, 16, 128), f32),
            dma((6,)), dma((2 * tiles,)), dma((chunks,)), dma((chunks,)), dma((2,)),
            dma, dma((chunks,)), dma, dma((chunks,)),
            dma((4,)), dma((4,)), dma((2,)), dma((2,)), dma((2,)), dma((2,)),
        ],
        compiler_params=pltpu.CompilerParams(
            collective_id=0, has_side_effects=True, vmem_limit_bytes=LIMIT << 20
        ),
        name="exchange",
    )(
        *[
            pltpu.with_memory_space_constraint(jnp.asarray(x), pltpu.HBM)
            for x in (state, direction, diffusivity, inverses, table_hi, table_lo, turns, weights, geometry)
        ]
    )
    return pl.pallas_call(
        functools.partial(finish_kernel, members, chunks),
        out_shape=(jax.ShapeDtypeStruct(state.shape, f32),) * 2,
        in_specs=[on_chip] * 6 + [pl.BlockSpec(memory_space=pltpu.HBM)],
        out_specs=(anywhere,) * 2,
        scratch_shapes=[
            pltpu.VMEM((levels, tiles, members * 24, 128), f32),
            pltpu.VMEM(geometry.shape[1:], f32),
            dma, dma((tiles,)), dma((tiles, members)), dma((tiles, members)),
        ],
        compiler_params=pltpu.CompilerParams(vmem_limit_bytes=8 << 20),
        name="finish",
    )(*parts, geometry)


def solution(mesh):
    return jax.shard_map(
        functools.partial(on_device, mesh.shape["lat"], mesh.shape["lon"]),
        mesh=mesh,
        in_specs=(
            P(None, "lat", "lon"),
            P(None, "lat", "lon"),
            P("lat", "lon"),
            P(("lat", "lon"), None, None, None, None),
        ),
        out_specs=(P(None, "lat", "lon"), P(None, "lat", "lon")),
        check_vma=False,
    )
```

```python
import functools
import math
import jax
import jax.numpy as jnp
import ml_dtypes
import numpy as np
from jax import lax
from jax.experimental import pallas as pl
from jax.experimental.pallas import tpu as pltpu
from jax.sharding import PartitionSpec as P

OUTER = 24
INNER = 512
HALF = 256


def real_dft(xs):
    n = len(xs)
    if n == 3:
        a, b, c = xs
        t = b + c
        return [(a + t, None), (a - 0.5 * t, (c - b) * math.sin(math.pi / 3))]
    even, odd = (real_dft(xs[0::2]), real_dft(xs[1::2]))
    half = n // 2
    out = [None] * (half + 1)
    out[0] = (even[0][0] + odd[0][0], None)
    out[half] = (even[0][0] - odd[0][0], None)
    for k in range(1, (half + 1) // 2):
        (er, ei), (pr, pi) = (even[k], odd[k])
        c, s = (math.cos(2 * math.pi * k / n), math.sin(2 * math.pi * k / n))
        tr, ti = (pr * c + pi * s, pi * c - pr * s)
        out[k] = (er + tr, ei + ti)
        out[half - k] = (er - tr, ti - ei)
    if half % 2 == 0:
        out[half // 2] = (even[half // 2][0], -odd[half // 2][0])
    return out


def real_dft_back(zs, n):
    if n == 3:
        (c, _), (e, o) = zs
        t, u = (c - 0.5 * e, o * math.sin(math.pi / 3))
        return [c + e, t - u, t + u]
    half = n // 2
    quarter = half // 2
    even = [(zs[0][0] + zs[half][0], None)]
    odd = [(zs[0][0] - zs[half][0], None)]
    for k in range(1, (half + 1) // 2):
        (er, ei), (pr, pi) = (zs[k], zs[half - k])
        even.append((er + pr, ei - pi))
        dr, di = (er - pr, ei + pi)
        c, s = (math.cos(2 * math.pi * k / n), math.sin(2 * math.pi * k / n))
        odd.append((dr * c - di * s, dr * s + di * c))
    if half % 2 == 0:
        even.append((zs[quarter][0], None))
        odd.append((-zs[quarter][1], None))
    first, second = (real_dft_back(even, half), real_dft_back(odd, half))
    return [v for pair in zip(first, second) for v in pair]


def make_tables():
    length = OUTER * INNER
    b = np.arange(INNER)
    q = np.arange(HALF)
    angle = 2 * np.pi * ((b[:, None] * q[None, :]) % INNER) / INNER
    c, s = (np.cos(angle), np.sin(angle))
    table = np.block([[c, -s], [s, c]])
    high = table.astype(ml_dtypes.bfloat16)
    low = (table - high.astype(np.float64)).astype(ml_dtypes.bfloat16)
    twist = 2 * np.pi * ((np.arange(OUTER)[:, None] * b[None, :]) % length) / length
    scale = 2.0 / length
    turns = np.stack(
        [np.cos(twist), np.sin(twist), scale * np.cos(twist), scale * np.sin(twist)]
    ).astype(np.float32)
    weights = np.ones((OUTER, HALF), np.float32)
    weights[0, 0] = 0.5
    return high, low, turns, weights


def split(x):
    high = x.astype(jnp.bfloat16)
    return high, (x - high.astype(jnp.float32)).astype(jnp.bfloat16)


def spectral_chunk(inb, outb, invb, table_hi, table_lo, turns, weights, wide, high, low, narrow, invf):
    levels = 2
    rows = 8

    def widen(k, _):
        invf[k] = invb[k // rows, k % rows].astype(jnp.float32) * weights[...]
        return 0

    lax.fori_loop(0, rows * rows, widen, 0)

    def stage_in(t, _):
        level, tile = (t // 4, t % 4)
        lane = pl.multiple_of(tile * 128, 128)
        xs = [inb[level, :, pl.ds(a * INNER + lane, 128)] for a in range(OUTER)]
        ys = real_dft(xs)
        for p in range(OUTER):
            m = p if p <= OUTER // 2 else OUTER - p
            re, im = ys[m]
            c = turns[0, pl.ds(p, 1), pl.ds(lane, 128)]
            s = turns[1, pl.ds(p, 1), pl.ds(lane, 128)]
            if im is None:
                tr, ti = (re * c, -(re * s))
            elif p <= OUTER // 2:
                tr, ti = (re * c + im * s, im * c - re * s)
            else:
                tr, ti = (re * c - im * s, -(im * c) - re * s)
            where = pl.ds(level * (rows * OUTER) + p, rows, stride=OUTER)
            wide[tile, where, :] = tr
            wide[tile + 4, where, :] = ti
        return 0

    lax.fori_loop(0, 8, stage_in, 0)

    def split_wide(k, _):
        at = pl.ds(pl.multiple_of(k * 32, 32), 32)
        for j in range(8):
            cols = slice(j * 128, j * 128 + 128)
            high[at, cols], low[at, cols] = split(wide[j, at, :])
        return 0

    lax.fori_loop(0, 12, split_wide, 0)

    def forward(n, _):
        cols = pl.ds(pl.multiple_of(n * 256, 256), 256)
        a = jnp.dot(high[...], table_hi[:, cols], preferred_element_type=jnp.float32)
        a += jnp.dot(low[...], table_hi[:, cols], preferred_element_type=jnp.float32)
        a += jnp.dot(high[...], table_lo[:, cols], preferred_element_type=jnp.float32)
        narrow[:, cols] = a
        return 0

    lax.fori_loop(0, 2, forward, 0)

    def solve(t, _):
        pt, lane = (pl.multiple_of((t // 2) * 8, 8), pl.multiple_of((t % 2) * 128, 128))
        spec = [
            [
                narrow[pl.ds((level * rows + s) * OUTER + pt, 8), pl.ds(part * HALF + lane, 128)]
                for level in range(levels)
                for part in range(2)
            ]
            for s in range(rows)
        ]
        for r in range(rows):
            total = [None] * 4
            for s in range(rows):
                factor = invf[r * rows + s, pl.ds(pt, 8), pl.ds(lane, 128)]
                for i in range(4):
                    term = factor * spec[s][i]
                    total[i] = term if total[i] is None else total[i] + term
            for i in range(4):
                level, part = (i // 2, i % 2)
                wide[part * 2 + t % 2, pl.ds((level * rows + r) * OUTER + pt, 8), :] = total[i]
        return 0

    lax.fori_loop(0, 6, solve, 0)

    def split_solved(k, _):
        at = pl.ds(pl.multiple_of(k * 32, 32), 32)
        for j in range(4):
            cols = slice(j * 128, j * 128 + 128)
            high[at, cols], low[at, cols] = split(wide[j, at, :])
        return 0

    lax.fori_loop(0, 12, split_solved, 0)

    def backward(n, _):
        cols = pl.ds(pl.multiple_of(n * 256, 256), 256)
        dims = (((1,), (1,)), ((), ()))
        hi, lo = (high[:, : 2 * HALF], low[:, : 2 * HALF])
        a = lax.dot_general(hi, table_hi[cols, :], dims, preferred_element_type=jnp.float32)
        a += lax.dot_general(lo, table_hi[cols, :], dims, preferred_element_type=jnp.float32)
        a += lax.dot_general(hi, table_lo[cols, :], dims, preferred_element_type=jnp.float32)
        wide[2 * n] = a[:, :128]
        wide[2 * n + 1] = a[:, 128:]
        return 0

    lax.fori_loop(0, 4, backward, 0)

    def stage_out(t, _):
        level, tile = (t // 4, t % 4)
        lane = pl.multiple_of(tile * 128, 128)

        def turned(p):
            where = pl.ds(level * (rows * OUTER) + p, rows, stride=OUTER)
            re = wide[tile, where, :]
            im = wide[tile + 4, where, :]
            c = turns[2, pl.ds(p, 1), pl.ds(lane, 128)]
            s = turns[3, pl.ds(p, 1), pl.ds(lane, 128)]
            return re * c - im * s, re * s + im * c

        zs = []
        for p in range(OUTER // 2 + 1):
            re, im = turned(p)
            if 0 < p < OUTER // 2:
                other_re, other_im = turned(OUTER - p)
                re, im = (re + other_re, im - other_im)
            zs.append((re, im))
        for a, v in enumerate(real_dft_back(zs, OUTER)):
            outb[level, a * (INNER // 128) + tile] = v
        return 0

    lax.fori_loop(0, 8, stage_out, 0)


zonal_tau = 0.1
merid_tau = 0.5
zonal_cap = 16.0
quad_coef = 0.25
step_size = 0.01
LIMIT = 36
GROUP = 4
MESH = pl.DeviceIdType.MESH


def make_geometry(bands, members, rows_each):
    total = bands * members * rows_each
    row = np.arange(total, dtype=np.float64)
    cell = np.sin(np.pi * (row + 0.5) / total)
    low = np.where(row > 0, np.sin(np.pi * row / total), 0.0)
    high = np.where(row + 1 < total, np.sin(np.pi * (row + 1) / total), 0.0)
    zonal = zonal_tau * np.minimum(1.0 / (cell * cell), zonal_cap)
    kinds = np.stack([zonal, merid_tau * high / cell, merid_tau * low / cell], -1)
    kinds = (0.25 * quad_coef) * kinds.reshape(bands, members, rows_each, 3)
    table = np.zeros((bands, rows_each + members, members, 8), np.float32)
    table[:, :rows_each, :, :3] = kinds.transpose(0, 2, 1, 3)
    table = table.reshape(bands, rows_each + members, members * 8)
    table[:, rows_each:, 0] = kinds[:, :, rows_each - 17, 1]
    table[:, rows_each:, 1] = kinds[:, :, rows_each - 8, 2]
    return table


def face(a, b, pa, pb):
    s, p, d, dp = (a + b, pa + pb, b - a, pb - pa)
    moved = s + step_size * p
    return (4.0 / quad_coef + moved * moved) * dp + p * (s + moved) * d


def align_halo(packed, aligned):
    rows = 8
    row = lax.broadcasted_iota(jnp.int32, (rows, 128), 0)

    def one(j, _):
        for level in range(packed.shape[1]):
            x = jnp.broadcast_to(packed[j, level : level + 1, :], (rows, 128))
            for bit in (1, 2, 4):
                x = jnp.where((row // bit) % 2 == 1, pltpu.roll(x, 128 - bit, 1), x)
            aligned[j, level] = x
        return 0

    lax.fori_loop(0, packed.shape[0], one, 0, unroll=True)


def stencil_tile(j, c, chunks, field, pre, kappa, scol, pcol, geometry, jac, skip="", target=None):
    levels, tiles = field.shape[:2]
    rows = 8
    line = pl.multiple_of((j * chunks + c) * rows, rows)
    base = line + rows
    own = pl.ds(pl.multiple_of(c * rows, rows), rows)
    target = line if target is None else pl.multiple_of(target, rows)
    lane = lax.broadcasted_iota(jnp.int32, (rows, 128), 1)
    first, last = (lane == 0, lane == 127)
    row = lax.broadcasted_iota(jnp.int32, (rows, 128), 0)
    geo = pltpu.roll(geometry[own, :], lax.rem(128 - 8 * j, 128), 1)
    zonal, above, below = [jnp.broadcast_to(geo[:, i : i + 1], (rows, 128)) for i in range(3)]

    def to_end(tile, at):
        return pltpu.roll(tile, lax.rem(255 - at, 128), 1)

    for level in range(levels):
        side = slice(level * rows, level * rows + rows)
        w = [field[level, k, pl.ds(base, rows), :] for k in range(tiles)]
        p = [pre[level, k, pl.ds(base, rows), :] for k in range(tiles)]
        rw = [pltpu.roll(x, 127, 1) for x in w] + [to_end(scol[1, side, :], 8 * j + c)]
        rp = [pltpu.roll(x, 127, 1) for x in p] + [to_end(pcol[j, level], (c * 2 + 1) * rows)]
        edge = face(
            to_end(scol[0, side, :], 8 * j + c), rw[0], to_end(pcol[j, level], c * 2 * rows), rp[0]
        )
        behind = pltpu.roll(edge, 1, 1)
        for k in range(tiles):
            east = face(
                w[k], jnp.where(last, rw[k + 1], rw[k]), p[k], jnp.where(last, rp[k + 1], rp[k])
            )
            turned = pltpu.roll(east, 1, 1)
            west = jnp.where(first, behind, turned)
            behind = turned
            if skip == "north":
                p_north = pltpu.roll(p[k], rows - 1, 0)
            else:
                p_north = pre[level, k, pl.ds(base + 1, rows), :]
            if skip == "south":
                p_south = pltpu.roll(p[k], 1, 0)
            else:
                p_south = pre[level, k, pl.ds(base - 1, rows), :]
            north = above * face(w[k], field[level, k, pl.ds(base + 1, rows), :], p[k], p_north)
            south = below * face(field[level, k, pl.ds(base - 1, rows), :], w[k], p_south, p[k])
            if skip == "north":
                north = jnp.where(row == rows - 1, 0.0, north)
            if skip == "south":
                south = jnp.where(row == 0, 0.0, south)
            spread = zonal * (east - west) + (north - south)
            jac[level, k, pl.ds(target, rows), :] = p[k] - kappa[k, pl.ds(line, rows), :] * spread


def exchange_kernel(
    bands, members, chunks,
    state, direction, diffusivity, inverses, table_hi_in, table_lo_in, turns_in, weights_in, geometry_in,
    field, pre, jac, kappa, scol, pcol, geometry,
    inb, outb, invb, table_hi, table_lo, turns, weights, kappa_in,
    wide, high, low, narrow, invf, scol_out, pcol_out, row_out, row_in, aligned,
    load_sem, field_sem, own_in, own_out, own_col, send_in, recv_in, send_out, recv_out,
    send_row, recv_row, send_col, recv_col, send_halo, recv_halo,
):
    levels, local_rows, width = state.shape
    rows = 8
    tiles = width // 128
    share = chunks * rows
    la, me = (lax.axis_index("lat"), lax.axis_index("lon"))
    up, down = (lax.rem(la + 1, bands), lax.rem(la + bands - 1, bands))
    east, west = (lax.rem(me + 1, members), lax.rem(me + members - 1, members))

    def peer(k):
        y = lax.rem(me // 4 + k // 4, members // 4)
        x = lax.rem(me // 2 + k // 2, 2)
        core = lax.rem(me + k, 2)
        return y * 4 + x * 2 + core

    def remote(src, dst, send, recv, lat, lon):
        return pltpu.make_async_remote_copy(
            src_ref=src, dst_ref=dst, send_sem=send, recv_sem=recv,
            device_id=(lat, lon), device_id_type=MESH,
        )

    barrier = pltpu.get_barrier_semaphore()
    for k in range(1, members):
        pl.semaphore_signal(barrier, inc=1, device_id=(la, peer(k)), device_id_type=MESH)
    for lat in (up, down):
        pl.semaphore_signal(barrier, inc=1, device_id=(lat, me), device_id_type=MESH)

    field_copies = [
        pltpu.make_async_copy(
            state.at[:, :, pl.ds(k * 128, 128)], field.at[:, k, pl.ds(rows, local_rows), :], field_sem.at[k]
        )
        for k in range(tiles)
    ]
    kappa_copies = [
        pltpu.make_async_copy(diffusivity.at[:, pl.ds(k * 128, 128)], kappa_in.at[k], field_sem.at[tiles + k])
        for k in range(tiles)
    ]
    loads = [
        pltpu.make_async_copy(src, dst, load_sem.at[i])
        for i, (src, dst) in enumerate(
            (
                (table_hi_in, table_hi), (table_lo_in, table_lo), (turns_in, turns),
                (weights_in, weights), (inverses, invb), (geometry_in.at[la], geometry),
            )
        )
    ]
    for copy in field_copies + loads + kappa_copies:
        copy.start()
    pl.semaphore_wait(barrier, members + 1)

    def chunk_of(i):
        return lax.rem(i + chunks - 1, chunks)

    def lines(member, c):
        return pl.ds(pl.multiple_of(member * share + c * rows, rows), rows)

    def landing(member, c):
        return pl.ds(pl.multiple_of(member * share + c * rows + rows, rows), rows)

    def columns(member):
        return pl.ds(pl.multiple_of(member * width, width), width)

    def send_inputs(i, _):
        c = chunk_of(i)
        for k in range(1, members):
            p = peer(k)
            remote(
                direction.at[:, lines(p, c), :], inb.at[c, :, :, columns(me)],
                send_in, recv_in.at[c], la, p,
            ).start()
        pltpu.make_async_copy(
            direction.at[:, lines(me, c), :], inb.at[c, :, :, columns(me)], own_in.at[c]
        ).start()
        return 0

    lax.fori_loop(0, chunks, send_inputs, 0)

    lane = lax.broadcasted_iota(jnp.int32, (rows, 128), 1)
    row = lax.broadcasted_iota(jnp.int32, (rows, 128), 0)
    for copy in field_copies:
        copy.wait()
    scol_out[...] = jnp.zeros_like(scol_out)

    def pack_state(t, _):
        at = (t // chunks) * 8 + lax.rem(t, chunks)
        for side, (k, spot) in enumerate(((0, 0), (tiles - 1, 127))):
            for level in range(levels):
                value = field[level, k, pl.ds(pl.multiple_of(t * rows + rows, rows), rows), :]
                value = pltpu.roll(value, lax.rem(at + 128 - spot, 128), 1)
                line = pl.ds(level * rows, rows)
                scol_out[side, line, :] = jnp.where(lane == at, value, scol_out[side, line, :])
        return 0

    lax.fori_loop(0, members * chunks, pack_state, 0)
    row_out[...] = jnp.zeros_like(row_out)

    def pack_row(source, line, slot):
        for level in range(levels):
            for k in range(tiles):
                at = level * tiles + k
                row_out[slot, at : at + 1, :] = source[level, k, line : line + 1, :]

    def unpack_row(target, line, slot):
        for level in range(levels):
            for k in range(tiles):
                at = level * tiles + k
                target[level, k, line : line + 1, :] = row_in[slot, at : at + 1, :]

    def row_copy(slot, lat):
        return remote(row_out.at[slot], row_in.at[slot], send_row.at[slot], recv_row.at[slot], lat, me)

    top, bottom = (rows + local_rows - 1, rows)
    pack_row(field, top, 0)
    pack_row(field, bottom, 1)
    pcol_out[...] = jnp.zeros_like(pcol_out)
    small = [
        remote(scol_out.at[1], scol.at[0], send_col.at[0], recv_col.at[0], la, east),
        remote(scol_out.at[0], scol.at[1], send_col.at[1], recv_col.at[1], la, west),
        row_copy(0, up),
        row_copy(1, down),
    ]
    for copy in small:
        copy.start()
    for copy in kappa_copies:
        copy.wait()

    def widen_kappa(t, _):
        at = pl.ds(pl.multiple_of(t * 32, 32), 32)
        for k in range(tiles):
            kappa[k, at, :] = kappa_in[k, at, :].astype(jnp.float32)
        return 0

    lax.fori_loop(0, local_rows // 32, widen_kappa, 0)
    for copy in loads:
        copy.wait()

    def chunk(i, _):
        c = chunk_of(i)
        part = inb.at[c, :, :, pl.ds(0, (members - 1) * width)]
        pltpu.make_async_copy(part, part, recv_in.at[c]).wait()
        pltpu.make_async_copy(
            direction.at[:, lines(me, c), :], inb.at[c, :, :, columns(me)], own_in.at[c]
        ).wait()
        spectral_chunk(
            inb.at[c], outb.at[c], invb.at[c], table_hi, table_lo, turns, weights,
            wide, high, low, narrow, invf,
        )

        slot = i // (chunks - 1)

        def pack(d, _):
            before = lax.rem(d * tiles + members * tiles - 1, members * tiles)
            after = lax.rem(d * tiles + tiles, members * tiles)
            for level in range(levels):
                held = jnp.zeros((rows, 128), jnp.float32)
                for side, (source, spot) in enumerate(((before, 127), (after, 0))):
                    value = jnp.broadcast_to(outb[c, level, source][:, spot : spot + 1], (rows, 128))
                    held = jnp.where(lane == (c * 2 + side) * rows + row, value, held)
                pcol_out[slot, d, level : level + 1, :] += jnp.sum(held, 0, keepdims=True)
            return 0

        lax.fori_loop(0, members, pack, 0)

        @pl.when(i >= chunks - 2)
        def _():
            for k in range(1, members):
                p = peer(k)
                remote(
                    pcol_out.at[slot, p], pcol.at[slot, me], send_halo.at[slot], recv_halo.at[slot], la, p
                ).start()
            pltpu.make_async_copy(pcol_out.at[slot, me], pcol.at[slot, me], own_col.at[slot]).start()

        for k in range(1, members):
            p = peer(k)
            remote(
                outb.at[c, :, pl.ds(p * tiles, tiles)], pre.at[:, :, landing(me, c), :],
                send_out, recv_out.at[c], la, p,
            ).start()
        pltpu.make_async_copy(
            outb.at[c, :, pl.ds(me * tiles, tiles)], pre.at[:, :, landing(me, c), :], own_out.at[c]
        ).start()
        return 0

    lax.fori_loop(0, chunks, chunk, 0)

    def landed(c):
        part = outb.at[c, :, pl.ds(0, (members - 1) * tiles)]
        pltpu.make_async_copy(part, part, recv_out.at[c]).wait()
        pltpu.make_async_copy(
            outb.at[c, :, pl.ds(me * tiles, tiles)], pre.at[:, :, landing(me, c), :], own_out.at[c]
        ).wait()

    def stencil(c, low, high, skip=""):
        def one(j, _):
            stencil_tile(j, c, chunks, field, pre, kappa, scol, aligned, geometry, jac, skip)
            return 0

        lax.fori_loop(low, high, one, 0)

    def halo(slot):
        others = pcol_out.at[slot, pl.ds(0, members - 1)]
        pltpu.make_async_copy(others, others, recv_halo.at[slot]).wait()
        pltpu.make_async_copy(pcol_out.at[slot, me], pcol.at[slot, me], own_col.at[slot]).wait()
        pltpu.make_async_copy(others, others, send_halo.at[slot]).wait()

    final = chunks - 1
    for copy in small:
        copy.wait()
    unpack_row(field, bottom - 1, 0)
    unpack_row(field, top + 1, 1)
    landed(final)
    pack_row(pre, top, 2)
    first = row_copy(2, up)
    first.start()
    landed(0)
    pack_row(pre, bottom, 3)
    second = row_copy(3, down)
    second.start()
    for c in range(1, chunks - 3):
        landed(c)
    halo(0)
    align_halo(pcol.at[0], aligned)
    stencil(0, 1, members)
    lax.fori_loop(1, chunks - 4, lambda c, _: (stencil(c, 0, members), 0)[1], 0)
    stencil(final, 0, members - 1, "south")
    landed(chunks - 3)
    stencil(chunks - 4, 0, members)
    stencil(chunks - 3, 0, members, "north")
    first.wait()
    second.wait()
    unpack_row(pre, bottom - 1, 2)
    unpack_row(pre, top + 1, 3)
    stencil(0, 0, 1)
    stencil(final, members - 1, members, "south")
    landed(chunks - 2)
    halo(1)
    part = inb.at[:, :, :, pl.ds(0, (members - 1) * width)]
    pltpu.make_async_copy(part, part, send_in).wait()
    part = outb.at[:, :, pl.ds(0, (members - 1) * tiles)]
    pltpu.make_async_copy(part, part, send_out).wait()


def finish_kernel(
    members, chunks, field, pre, jac, kappa, scol, pcol, geometry,
    pre_out, jac_out, work, aligned, pre_sem, early_sem, late_sem,
):
    levels, tiles = field.shape[:2]
    rows = 8
    share = chunks * rows
    late = 3 * rows
    early = share - late
    count = members * share

    def lane_tile(k):
        return pl.ds(k * 128, 128)

    pre_copies = [
        pltpu.make_async_copy(
            pre.at[:, k, pl.ds(rows, count), :], pre_out.at[:, :, lane_tile(k)], pre_sem.at[k]
        )
        for k in range(tiles)
    ]

    shape = (levels, tiles, members)
    jac_parts = jac.reshape(*shape, share, 128)
    work_parts = work.reshape(*shape, late, 128)
    out_parts = jac_out.reshape(levels, members, share, tiles * 128)
    early_copies = [
        pltpu.make_async_copy(
            jac_parts.at[:, k, :, :early, :], out_parts.at[:, :, :early, lane_tile(k)], early_sem.at[k]
        )
        for k in range(tiles)
    ]

    def late_copy(q, k):
        some = pl.ds(q * GROUP, GROUP)
        return pltpu.make_async_copy(
            work_parts.at[:, k, some], out_parts.at[:, some, early:, lane_tile(k)], late_sem.at[q, k]
        )

    for copy in pre_copies + early_copies:
        copy.start()

    align_halo(pcol.at[1], aligned)

    def group(g, _):
        def take(j, _):
            for level in range(levels):
                for k in range(tiles):
                    for at in (0, late - rows):
                        source = pl.ds(pl.multiple_of(j * share + early + at, rows), rows)
                        target = pl.ds(pl.multiple_of(j * late + at, rows), rows)
                        work[level, k, target, :] = jac[level, k, source, :]
            return 0

        lax.fori_loop(g * rows, g * rows + rows, take, 0)
        factor = geometry[pl.ds(pl.multiple_of(share + g * rows, rows), rows), :]
        above, below = [jnp.broadcast_to(factor[:, i : i + 1], (rows, 128)) for i in range(2)]

        def every(at, padded=0):
            return pl.ds(g * rows * share + early + at + padded, rows, stride=share)

        for level in range(levels):
            for k in range(tiles):
                def pair(at):
                    lower, upper = (every(at, rows), every(at + 1, rows))
                    return face(field[level, k, lower, :], field[level, k, upper, :], pre[level, k, lower, :], pre[level, k, upper, :])

                low_at, high_at = (rows - 1, late - rows)
                fixed = jac[level, k, every(low_at), :] - kappa[k, every(low_at), :] * (above * pair(low_at))
                work[level, k, pl.ds(g * rows * late + low_at, rows, stride=late), :] = fixed
                fixed = jac[level, k, every(high_at), :] + kappa[k, every(high_at), :] * (below * pair(high_at - 1))
                work[level, k, pl.ds(g * rows * late + high_at, rows, stride=late), :] = fixed

        def one(j, _):
            stencil_tile(
                j, chunks - 2, chunks, field, pre, kappa, scol, aligned, geometry,
                work, "", j * late + rows,
            )
            return 0

        def some(q, _):
            lax.fori_loop(q * GROUP, q * GROUP + GROUP, one, 0)
            for k in range(tiles):
                late_copy(q, k).start()
            return 0

        lax.fori_loop(g * (rows // GROUP), (g + 1) * (rows // GROUP), some, 0)
        return 0

    lax.fori_loop(0, members // rows, group, 0)

    def drain(q, _):
        for k in range(tiles):
            late_copy(q, k).wait()
        return 0

    lax.fori_loop(0, members // GROUP, drain, 0)
    for copy in pre_copies + early_copies:
        copy.wait()


def on_device(bands, members, state, direction, diffusivity, inverses):
    levels, local_rows, width = state.shape
    chunks = inverses.shape[0]
    tiles = width // 128
    share = local_rows // members
    table_hi, table_lo, turns, weights = make_tables()
    geometry = jnp.asarray(make_geometry(bands, members, share))
    f32 = jnp.float32
    anywhere = pl.BlockSpec(memory_space=pl.ANY)
    on_chip = pl.BlockSpec(memory_space=pltpu.VMEM)
    dma = pltpu.SemaphoreType.DMA
    padded = (levels, tiles, local_rows + 16, 128)
    parts = pl.pallas_call(
        functools.partial(exchange_kernel, bands, members, chunks),
        out_shape=(
            pltpu.VMEM(padded, f32),
            pltpu.VMEM(padded, f32),
            pltpu.VMEM((levels, tiles, local_rows, 128), f32),
            pltpu.VMEM((tiles, local_rows, 128), f32),
            pltpu.VMEM((2, levels * 8, 128), f32),
            pltpu.VMEM((2, members, levels, 128), f32),
            pltpu.VMEM(geometry.shape[1:], f32),
        ),
        in_specs=[pl.BlockSpec(memory_space=pltpu.HBM)] * 9,
        out_specs=(on_chip,) * 7,
        scratch_shapes=[
            pltpu.VMEM((chunks, levels, 8, members * width), f32),
            pltpu.VMEM((chunks, levels, members * tiles, 8, 128), f32),
            pltpu.VMEM(inverses.shape, jnp.bfloat16),
            pltpu.VMEM(table_hi.shape, jnp.bfloat16),
            pltpu.VMEM(table_lo.shape, jnp.bfloat16),
            pltpu.VMEM(turns.shape, f32),
            pltpu.VMEM(weights.shape, f32),
            pltpu.VMEM((tiles, local_rows, 128), jnp.bfloat16),
            pltpu.VMEM((8, levels * 8 * OUTER, 128), f32),
            pltpu.VMEM((levels * 8 * OUTER, 2 * INNER), jnp.bfloat16),
            pltpu.VMEM((levels * 8 * OUTER, 2 * INNER), jnp.bfloat16),
            pltpu.VMEM((levels * 8 * OUTER, INNER), f32),
            pltpu.VMEM((64, OUTER, HALF), f32),
            pltpu.VMEM((2, levels * 8, 128), f32),
            pltpu.VMEM((2, members, levels, 128), f32),
            pltpu.VMEM((4, 16, 128), f32),
            pltpu.VMEM((4, 16, 128), f32),
            pltpu.VMEM((members, levels, 8, 128), f32),
            dma((6,)), dma((2 * tiles,)), dma((chunks,)), dma((chunks,)), dma((2,)),
            dma, dma((chunks,)), dma, dma((chunks,)),
            dma((4,)), dma((4,)), dma((2,)), dma((2,)), dma((2,)), dma((2,)),
        ],
        compiler_params=pltpu.CompilerParams(
            collective_id=0, has_side_effects=True, vmem_limit_bytes=LIMIT << 20
        ),
        name="exchange",
    )(
        *[
            pltpu.with_memory_space_constraint(jnp.asarray(x), pltpu.HBM)
            for x in (state, direction, diffusivity, inverses, table_hi, table_lo, turns, weights, geometry)
        ]
    )
    return pl.pallas_call(
        functools.partial(finish_kernel, members, chunks),
        out_shape=(jax.ShapeDtypeStruct(state.shape, f32),) * 2,
        in_specs=[on_chip] * 7,
        out_specs=(anywhere,) * 2,
        scratch_shapes=[
            pltpu.VMEM((levels, tiles, members * 24, 128), f32),
            pltpu.VMEM((members, levels, 8, 128), f32),
            dma((tiles,)), dma((tiles,)), dma((members // GROUP, tiles)),
        ],
        compiler_params=pltpu.CompilerParams(vmem_limit_bytes=8 << 20),
        name="finish",
    )(*parts)


def solution(mesh):
    return jax.shard_map(
        functools.partial(on_device, mesh.shape["lat"], mesh.shape["lon"]),
        mesh=mesh,
        in_specs=(
            P(None, "lat", "lon"),
            P(None, "lat", "lon"),
            P("lat", "lon"),
            P(("lat", "lon"), None, None, None, None),
        ),
        out_specs=(P(None, "lat", "lon"), P(None, "lat", "lon")),
        check_vma=False,
    )
```

```python
import functools
import math
import jax
import jax.numpy as jnp
import ml_dtypes
import numpy as np
from jax import lax
from jax.experimental import pallas as pl
from jax.experimental.pallas import tpu as pltpu
from jax.sharding import PartitionSpec as P

OUTER = 24
INNER = 512
HALF = 256


def real_dft(xs):
    n = len(xs)
    if n == 3:
        a, b, c = xs
        t = b + c
        return [(a + t, None), (a - 0.5 * t, (c - b) * math.sin(math.pi / 3))]
    even, odd = (real_dft(xs[0::2]), real_dft(xs[1::2]))
    half = n // 2
    out = [None] * (half + 1)
    out[0] = (even[0][0] + odd[0][0], None)
    out[half] = (even[0][0] - odd[0][0], None)
    for k in range(1, (half + 1) // 2):
        (er, ei), (pr, pi) = (even[k], odd[k])
        c, s = (math.cos(2 * math.pi * k / n), math.sin(2 * math.pi * k / n))
        tr, ti = (pr * c + pi * s, pi * c - pr * s)
        out[k] = (er + tr, ei + ti)
        out[half - k] = (er - tr, ti - ei)
    if half % 2 == 0:
        out[half // 2] = (even[half // 2][0], -odd[half // 2][0])
    return out


def real_dft_back(zs, n):
    if n == 3:
        (c, _), (e, o) = zs
        t, u = (c - 0.5 * e, o * math.sin(math.pi / 3))
        return [c + e, t - u, t + u]
    half = n // 2
    quarter = half // 2
    even = [(zs[0][0] + zs[half][0], None)]
    odd = [(zs[0][0] - zs[half][0], None)]
    for k in range(1, (half + 1) // 2):
        (er, ei), (pr, pi) = (zs[k], zs[half - k])
        even.append((er + pr, ei - pi))
        dr, di = (er - pr, ei + pi)
        c, s = (math.cos(2 * math.pi * k / n), math.sin(2 * math.pi * k / n))
        odd.append((dr * c - di * s, dr * s + di * c))
    if half % 2 == 0:
        even.append((zs[quarter][0], None))
        odd.append((-zs[quarter][1], None))
    first, second = (real_dft_back(even, half), real_dft_back(odd, half))
    return [v for pair in zip(first, second) for v in pair]


def make_tables():
    length = OUTER * INNER
    b = np.arange(INNER)
    q = np.arange(HALF)
    angle = 2 * np.pi * ((b[:, None] * q[None, :]) % INNER) / INNER
    c, s = (np.cos(angle), np.sin(angle))
    table = np.block([[c, -s], [s, c]])
    high = table.astype(ml_dtypes.bfloat16)
    low = (table - high.astype(np.float64)).astype(ml_dtypes.bfloat16)
    twist = 2 * np.pi * ((np.arange(OUTER)[:, None] * b[None, :]) % length) / length
    scale = 2.0 / length
    turns = np.stack(
        [np.cos(twist), np.sin(twist), scale * np.cos(twist), scale * np.sin(twist)]
    ).astype(np.float32)
    weights = np.ones((OUTER, HALF), np.float32)
    weights[0, 0] = 0.5
    return high, low, turns, weights


def split(x):
    high = x.astype(jnp.bfloat16)
    return high, (x - high.astype(jnp.float32)).astype(jnp.bfloat16)


def spectral_chunk(inb, outb, invb, table_hi, table_lo, turns, weights, wide, high, low, narrow, invf):
    levels = 2
    rows = 8

    def widen(k, _):
        invf[k] = invb[k // rows, k % rows].astype(jnp.float32) * weights[...]
        return 0

    lax.fori_loop(0, rows * rows, widen, 0)

    def stage_in(t, _):
        level, tile = (t // 4, t % 4)
        lane = pl.multiple_of(tile * 128, 128)
        xs = [inb[level, :, pl.ds(a * INNER + lane, 128)] for a in range(OUTER)]
        ys = real_dft(xs)
        for p in range(OUTER):
            m = p if p <= OUTER // 2 else OUTER - p
            re, im = ys[m]
            c = turns[0, pl.ds(p, 1), pl.ds(lane, 128)]
            s = turns[1, pl.ds(p, 1), pl.ds(lane, 128)]
            if im is None:
                tr, ti = (re * c, -(re * s))
            elif p <= OUTER // 2:
                tr, ti = (re * c + im * s, im * c - re * s)
            else:
                tr, ti = (re * c - im * s, -(im * c) - re * s)
            where = pl.ds(level * (rows * OUTER) + p, rows, stride=OUTER)
            wide[tile, where, :] = tr
            wide[tile + 4, where, :] = ti
        return 0

    lax.fori_loop(0, 8, stage_in, 0)

    def split_wide(k, _):
        at = pl.ds(pl.multiple_of(k * 32, 32), 32)
        for j in range(8):
            cols = slice(j * 128, j * 128 + 128)
            high[at, cols], low[at, cols] = split(wide[j, at, :])
        return 0

    lax.fori_loop(0, 12, split_wide, 0)

    def forward(n, _):
        cols = pl.ds(pl.multiple_of(n * 256, 256), 256)
        a = jnp.dot(high[...], table_hi[:, cols], preferred_element_type=jnp.float32)
        a += jnp.dot(low[...], table_hi[:, cols], preferred_element_type=jnp.float32)
        a += jnp.dot(high[...], table_lo[:, cols], preferred_element_type=jnp.float32)
        narrow[:, cols] = a
        return 0

    lax.fori_loop(0, 2, forward, 0)

    def solve(t, _):
        pt, lane = (pl.multiple_of((t // 2) * 8, 8), pl.multiple_of((t % 2) * 128, 128))
        spec = [
            [
                narrow[pl.ds((level * rows + s) * OUTER + pt, 8), pl.ds(part * HALF + lane, 128)]
                for level in range(levels)
                for part in range(2)
            ]
            for s in range(rows)
        ]
        for r in range(rows):
            total = [None] * 4
            for s in range(rows):
                factor = invf[r * rows + s, pl.ds(pt, 8), pl.ds(lane, 128)]
                for i in range(4):
                    term = factor * spec[s][i]
                    total[i] = term if total[i] is None else total[i] + term
            for i in range(4):
                level, part = (i // 2, i % 2)
                wide[part * 2 + t % 2, pl.ds((level * rows + r) * OUTER + pt, 8), :] = total[i]
        return 0

    lax.fori_loop(0, 6, solve, 0)

    def split_solved(k, _):
        at = pl.ds(pl.multiple_of(k * 32, 32), 32)
        for j in range(4):
            cols = slice(j * 128, j * 128 + 128)
            high[at, cols], low[at, cols] = split(wide[j, at, :])
        return 0

    lax.fori_loop(0, 12, split_solved, 0)

    def backward(n, _):
        cols = pl.ds(pl.multiple_of(n * 256, 256), 256)
        dims = (((1,), (1,)), ((), ()))
        hi, lo = (high[:, : 2 * HALF], low[:, : 2 * HALF])
        a = lax.dot_general(hi, table_hi[cols, :], dims, preferred_element_type=jnp.float32)
        a += lax.dot_general(lo, table_hi[cols, :], dims, preferred_element_type=jnp.float32)
        a += lax.dot_general(hi, table_lo[cols, :], dims, preferred_element_type=jnp.float32)
        wide[2 * n] = a[:, :128]
        wide[2 * n + 1] = a[:, 128:]
        return 0

    lax.fori_loop(0, 4, backward, 0)

    def stage_out(t, _):
        level, tile = (t // 4, t % 4)
        lane = pl.multiple_of(tile * 128, 128)

        def turned(p):
            where = pl.ds(level * (rows * OUTER) + p, rows, stride=OUTER)
            re = wide[tile, where, :]
            im = wide[tile + 4, where, :]
            c = turns[2, pl.ds(p, 1), pl.ds(lane, 128)]
            s = turns[3, pl.ds(p, 1), pl.ds(lane, 128)]
            return re * c - im * s, re * s + im * c

        zs = []
        for p in range(OUTER // 2 + 1):
            re, im = turned(p)
            if 0 < p < OUTER // 2:
                other_re, other_im = turned(OUTER - p)
                re, im = (re + other_re, im - other_im)
            zs.append((re, im))
        for a, v in enumerate(real_dft_back(zs, OUTER)):
            outb[level, a * (INNER // 128) + tile] = v
        return 0

    lax.fori_loop(0, 8, stage_out, 0)


zonal_tau = 0.1
merid_tau = 0.5
zonal_cap = 16.0
quad_coef = 0.25
step_size = 0.01
LIMIT = 36
GROUP = 4
MESH = pl.DeviceIdType.MESH


def make_geometry(bands, members, rows_each):
    total = bands * members * rows_each
    row = np.arange(total, dtype=np.float64)
    cell = np.sin(np.pi * (row + 0.5) / total)
    low = np.where(row > 0, np.sin(np.pi * row / total), 0.0)
    high = np.where(row + 1 < total, np.sin(np.pi * (row + 1) / total), 0.0)
    zonal = zonal_tau * np.minimum(1.0 / (cell * cell), zonal_cap)
    kinds = np.stack([zonal, merid_tau * high / cell, merid_tau * low / cell], -1)
    kinds = (0.25 * quad_coef) * kinds.reshape(bands, members, rows_each, 3)
    table = np.zeros((bands, rows_each + members, members, 8), np.float32)
    table[:, :rows_each, :, :3] = kinds.transpose(0, 2, 1, 3)
    table = table.reshape(bands, rows_each + members, members * 8)
    table[:, rows_each:, 0] = kinds[:, :, rows_each - 17, 1]
    table[:, rows_each:, 1] = kinds[:, :, rows_each - 8, 2]
    return table


def face(a, b, pa, pb):
    s, p, d, dp = (a + b, pa + pb, b - a, pb - pa)
    moved = s + step_size * p
    return (4.0 / quad_coef + moved * moved) * dp + p * (s + moved) * d


def align_halo(packed, aligned):
    rows = 8
    row = lax.broadcasted_iota(jnp.int32, (rows, 128), 0)

    def one(j, _):
        for level in range(packed.shape[1]):
            x = jnp.broadcast_to(packed[j, level : level + 1, :], (rows, 128))
            for bit in (1, 2, 4):
                x = jnp.where((row // bit) % 2 == 1, pltpu.roll(x, 128 - bit, 1), x)
            aligned[j, level] = x
        return 0

    lax.fori_loop(0, packed.shape[0], one, 0, unroll=True)


def stencil_tile(j, c, chunks, field, pre, kappa, scol, pcol, geometry, jac, skip="", target=None):
    levels, tiles = field.shape[:2]
    rows = 8
    line = pl.multiple_of((j * chunks + c) * rows, rows)
    base = line + rows
    own = pl.ds(pl.multiple_of(c * rows, rows), rows)
    target = line if target is None else pl.multiple_of(target, rows)
    lane = lax.broadcasted_iota(jnp.int32, (rows, 128), 1)
    first, last = (lane == 0, lane == 127)
    row = lax.broadcasted_iota(jnp.int32, (rows, 128), 0)
    geo = pltpu.roll(geometry[own, :], lax.rem(128 - 8 * j, 128), 1)
    zonal, above, below = [jnp.broadcast_to(geo[:, i : i + 1], (rows, 128)) for i in range(3)]

    def to_end(tile, at):
        return pltpu.roll(tile, lax.rem(255 - at, 128), 1)

    for level in range(levels):
        side = slice(level * rows, level * rows + rows)
        w = [field[level, k, pl.ds(base, rows), :] for k in range(tiles)]
        p = [pre[level, k, pl.ds(base, rows), :] for k in range(tiles)]
        rw = [pltpu.roll(x, 127, 1) for x in w] + [to_end(scol[1, side, :], 8 * j + c)]
        rp = [pltpu.roll(x, 127, 1) for x in p] + [to_end(pcol[j, level], (c * 2 + 1) * rows)]
        edge = face(
            to_end(scol[0, side, :], 8 * j + c), rw[0], to_end(pcol[j, level], c * 2 * rows), rp[0]
        )
        behind = pltpu.roll(edge, 1, 1)
        for k in range(tiles):
            east = face(
                w[k], jnp.where(last, rw[k + 1], rw[k]), p[k], jnp.where(last, rp[k + 1], rp[k])
            )
            turned = pltpu.roll(east, 1, 1)
            west = jnp.where(first, behind, turned)
            behind = turned
            if skip == "north":
                p_north = pltpu.roll(p[k], rows - 1, 0)
            else:
                p_north = pre[level, k, pl.ds(base + 1, rows), :]
            if skip == "south":
                p_south = pltpu.roll(p[k], 1, 0)
            else:
                p_south = pre[level, k, pl.ds(base - 1, rows), :]
            north = above * face(w[k], field[level, k, pl.ds(base + 1, rows), :], p[k], p_north)
            south = below * face(field[level, k, pl.ds(base - 1, rows), :], w[k], p_south, p[k])
            if skip == "north":
                north = jnp.where(row == rows - 1, 0.0, north)
            if skip == "south":
                south = jnp.where(row == 0, 0.0, south)
            spread = zonal * (east - west) + (north - south)
            jac[level, k, pl.ds(target, rows), :] = p[k] - kappa[k, pl.ds(line, rows), :] * spread


def exchange_kernel(
    bands, members, chunks,
    state, direction, diffusivity, inverses, table_hi_in, table_lo_in, turns_in, weights_in, geometry_in,
    field, pre, jac, kappa, scol, aligned, geometry,
    inb, outb, invb, table_hi, table_lo, turns, weights, kappa_in,
    wide, high, low, narrow, invf, scol_out, pcol_out, row_out, row_in, pcol,
    load_sem, field_sem, own_in, own_out, own_col, send_in, recv_in, send_out, recv_out,
    send_row, recv_row, send_col, recv_col, send_halo, recv_halo,
):
    levels, local_rows, width = state.shape
    rows = 8
    tiles = width // 128
    share = chunks * rows
    la, me = (lax.axis_index("lat"), lax.axis_index("lon"))
    up, down = (lax.rem(la + 1, bands), lax.rem(la + bands - 1, bands))
    east, west = (lax.rem(me + 1, members), lax.rem(me + members - 1, members))

    def peer(k):
        y = lax.rem(me // 4 + k // 4, members // 4)
        x = lax.rem(me // 2 + k // 2, 2)
        core = lax.rem(me + k, 2)
        return y * 4 + x * 2 + core

    def remote(src, dst, send, recv, lat, lon):
        return pltpu.make_async_remote_copy(
            src_ref=src, dst_ref=dst, send_sem=send, recv_sem=recv,
            device_id=(lat, lon), device_id_type=MESH,
        )

    barrier = pltpu.get_barrier_semaphore()
    for k in range(1, members):
        pl.semaphore_signal(barrier, inc=1, device_id=(la, peer(k)), device_id_type=MESH)
    for lat in (up, down):
        pl.semaphore_signal(barrier, inc=1, device_id=(lat, me), device_id_type=MESH)

    field_copies = [
        pltpu.make_async_copy(
            state.at[:, :, pl.ds(k * 128, 128)], field.at[:, k, pl.ds(rows, local_rows), :], field_sem.at[k]
        )
        for k in range(tiles)
    ]
    kappa_copies = [
        pltpu.make_async_copy(diffusivity.at[:, pl.ds(k * 128, 128)], kappa_in.at[k], field_sem.at[tiles + k])
        for k in range(tiles)
    ]
    loads = [
        pltpu.make_async_copy(src, dst, load_sem.at[i])
        for i, (src, dst) in enumerate(
            (
                (table_hi_in, table_hi), (table_lo_in, table_lo), (turns_in, turns),
                (weights_in, weights), (inverses, invb), (geometry_in.at[la], geometry),
            )
        )
    ]
    for copy in field_copies + loads + kappa_copies:
        copy.start()
    pl.semaphore_wait(barrier, members + 1)

    def chunk_of(i):
        return lax.rem(i + chunks - 1, chunks)

    def lines(member, c):
        return pl.ds(pl.multiple_of(member * share + c * rows, rows), rows)

    def landing(member, c):
        return pl.ds(pl.multiple_of(member * share + c * rows + rows, rows), rows)

    def columns(member):
        return pl.ds(pl.multiple_of(member * width, width), width)

    def send_inputs(i, _):
        c = chunk_of(i)
        for k in range(1, members):
            p = peer(k)
            remote(
                direction.at[:, lines(p, c), :], inb.at[c, :, :, columns(me)],
                send_in, recv_in.at[c], la, p,
            ).start()
        pltpu.make_async_copy(
            direction.at[:, lines(me, c), :], inb.at[c, :, :, columns(me)], own_in.at[c]
        ).start()
        return 0

    lax.fori_loop(0, chunks, send_inputs, 0)

    lane = lax.broadcasted_iota(jnp.int32, (rows, 128), 1)
    row = lax.broadcasted_iota(jnp.int32, (rows, 128), 0)
    for copy in field_copies:
        copy.wait()
    scol_out[...] = jnp.zeros_like(scol_out)

    def pack_state(t, _):
        at = (t // chunks) * 8 + lax.rem(t, chunks)
        for side, (k, spot) in enumerate(((0, 0), (tiles - 1, 127))):
            for level in range(levels):
                value = field[level, k, pl.ds(pl.multiple_of(t * rows + rows, rows), rows), :]
                value = pltpu.roll(value, lax.rem(at + 128 - spot, 128), 1)
                line = pl.ds(level * rows, rows)
                scol_out[side, line, :] = jnp.where(lane == at, value, scol_out[side, line, :])
        return 0

    lax.fori_loop(0, members * chunks, pack_state, 0)
    row_out[...] = jnp.zeros_like(row_out)

    def pack_row(source, line, slot):
        for level in range(levels):
            for k in range(tiles):
                at = level * tiles + k
                row_out[slot, at : at + 1, :] = source[level, k, line : line + 1, :]

    def unpack_row(target, line, slot):
        for level in range(levels):
            for k in range(tiles):
                at = level * tiles + k
                target[level, k, line : line + 1, :] = row_in[slot, at : at + 1, :]

    def row_copy(slot, lat):
        return remote(row_out.at[slot], row_in.at[slot], send_row.at[slot], recv_row.at[slot], lat, me)

    top, bottom = (rows + local_rows - 1, rows)
    pack_row(field, top, 0)
    pack_row(field, bottom, 1)
    pcol_out[...] = jnp.zeros_like(pcol_out)
    small = [
        remote(scol_out.at[1], scol.at[0], send_col.at[0], recv_col.at[0], la, east),
        remote(scol_out.at[0], scol.at[1], send_col.at[1], recv_col.at[1], la, west),
        row_copy(0, up),
        row_copy(1, down),
    ]
    for copy in small:
        copy.start()
    for copy in kappa_copies:
        copy.wait()

    def widen_kappa(t, _):
        at = pl.ds(pl.multiple_of(t * 32, 32), 32)
        for k in range(tiles):
            kappa[k, at, :] = kappa_in[k, at, :].astype(jnp.float32)
        return 0

    lax.fori_loop(0, local_rows // 32, widen_kappa, 0)
    for copy in loads:
        copy.wait()

    def chunk(i, _):
        c = chunk_of(i)
        part = inb.at[c, :, :, pl.ds(0, (members - 1) * width)]
        pltpu.make_async_copy(part, part, recv_in.at[c]).wait()
        pltpu.make_async_copy(
            direction.at[:, lines(me, c), :], inb.at[c, :, :, columns(me)], own_in.at[c]
        ).wait()
        spectral_chunk(
            inb.at[c], outb.at[c], invb.at[c], table_hi, table_lo, turns, weights,
            wide, high, low, narrow, invf,
        )

        slot = i // (chunks - 1)

        def pack(d, _):
            before = lax.rem(d * tiles + members * tiles - 1, members * tiles)
            after = lax.rem(d * tiles + tiles, members * tiles)
            for level in range(levels):
                held = jnp.zeros((rows, 128), jnp.float32)
                for side, (source, spot) in enumerate(((before, 127), (after, 0))):
                    value = jnp.broadcast_to(outb[c, level, source][:, spot : spot + 1], (rows, 128))
                    held = jnp.where(lane == (c * 2 + side) * rows + row, value, held)
                pcol_out[slot, d, level : level + 1, :] += jnp.sum(held, 0, keepdims=True)
            return 0

        lax.fori_loop(0, members, pack, 0)

        @pl.when(i >= chunks - 2)
        def _():
            for k in range(1, members):
                p = peer(k)
                remote(
                    pcol_out.at[slot, p], pcol.at[slot, me], send_halo.at[slot], recv_halo.at[slot], la, p
                ).start()
            pltpu.make_async_copy(pcol_out.at[slot, me], pcol.at[slot, me], own_col.at[slot]).start()

        for k in range(1, members):
            p = peer(k)
            remote(
                outb.at[c, :, pl.ds(p * tiles, tiles)], pre.at[:, :, landing(me, c), :],
                send_out, recv_out.at[c], la, p,
            ).start()
        pltpu.make_async_copy(
            outb.at[c, :, pl.ds(me * tiles, tiles)], pre.at[:, :, landing(me, c), :], own_out.at[c]
        ).start()
        return 0

    lax.fori_loop(0, chunks, chunk, 0)

    def landed(c):
        part = outb.at[c, :, pl.ds(0, (members - 1) * tiles)]
        pltpu.make_async_copy(part, part, recv_out.at[c]).wait()
        pltpu.make_async_copy(
            outb.at[c, :, pl.ds(me * tiles, tiles)], pre.at[:, :, landing(me, c), :], own_out.at[c]
        ).wait()

    def stencil(c, low, high, skip=""):
        def one(j, _):
            stencil_tile(j, c, chunks, field, pre, kappa, scol, aligned, geometry, jac, skip)
            return 0

        lax.fori_loop(low, high, one, 0)

    def halo(slot):
        others = pcol_out.at[slot, pl.ds(0, members - 1)]
        pltpu.make_async_copy(others, others, recv_halo.at[slot]).wait()
        pltpu.make_async_copy(pcol_out.at[slot, me], pcol.at[slot, me], own_col.at[slot]).wait()
        pltpu.make_async_copy(others, others, send_halo.at[slot]).wait()

    final = chunks - 1
    for copy in small:
        copy.wait()
    unpack_row(field, bottom - 1, 0)
    unpack_row(field, top + 1, 1)
    landed(final)
    pack_row(pre, top, 2)
    first = row_copy(2, up)
    first.start()
    landed(0)
    pack_row(pre, bottom, 3)
    second = row_copy(3, down)
    second.start()
    for c in range(1, chunks - 3):
        landed(c)
    halo(0)
    align_halo(pcol.at[0], aligned)
    stencil(0, 1, members)
    lax.fori_loop(1, chunks - 4, lambda c, _: (stencil(c, 0, members), 0)[1], 0)
    stencil(final, 0, members - 1, "south")
    landed(chunks - 3)
    stencil(chunks - 4, 0, members)
    stencil(chunks - 3, 0, members, "north")
    first.wait()
    second.wait()
    unpack_row(pre, bottom - 1, 2)
    unpack_row(pre, top + 1, 3)
    stencil(0, 0, 1)
    stencil(final, members - 1, members, "south")
    halo(1)
    align_halo(pcol.at[1], aligned)
    landed(chunks - 2)
    part = inb.at[:, :, :, pl.ds(0, (members - 1) * width)]
    pltpu.make_async_copy(part, part, send_in).wait()
    part = outb.at[:, :, pl.ds(0, (members - 1) * tiles)]
    pltpu.make_async_copy(part, part, send_out).wait()


def finish_kernel(
    members, chunks, field, pre, jac, kappa, scol, aligned, geometry,
    pre_out, jac_out, work, pre_sem, early_sem, late_sem,
):
    levels, tiles = field.shape[:2]
    rows = 8
    share = chunks * rows
    late = 3 * rows
    early = share - late
    count = members * share

    def lane_tile(k):
        return pl.ds(k * 128, 128)

    pre_copies = [
        pltpu.make_async_copy(
            pre.at[:, k, pl.ds(rows, count), :], pre_out.at[:, :, lane_tile(k)], pre_sem.at[k]
        )
        for k in range(tiles)
    ]

    shape = (levels, tiles, members)
    jac_parts = jac.reshape(*shape, share, 128)
    work_parts = work.reshape(*shape, late, 128)
    out_parts = jac_out.reshape(levels, members, share, tiles * 128)
    early_copies = [
        pltpu.make_async_copy(
            jac_parts.at[:, k, :, :early, :], out_parts.at[:, :, :early, lane_tile(k)], early_sem.at[k]
        )
        for k in range(tiles)
    ]

    def late_copy(q, k):
        some = pl.ds(q * GROUP, GROUP)
        return pltpu.make_async_copy(
            work_parts.at[:, k, some], out_parts.at[:, some, early:, lane_tile(k)], late_sem.at[q, k]
        )

    for copy in pre_copies + early_copies:
        copy.start()

    def group(g, _):
        def take(j, _):
            for level in range(levels):
                for k in range(tiles):
                    for at in (0, late - rows):
                        source = pl.ds(pl.multiple_of(j * share + early + at, rows), rows)
                        target = pl.ds(pl.multiple_of(j * late + at, rows), rows)
                        work[level, k, target, :] = jac[level, k, source, :]
            return 0

        lax.fori_loop(g * rows, g * rows + rows, take, 0)
        factor = geometry[pl.ds(pl.multiple_of(share + g * rows, rows), rows), :]
        above, below = [jnp.broadcast_to(factor[:, i : i + 1], (rows, 128)) for i in range(2)]

        def every(at, padded=0):
            return pl.ds(g * rows * share + early + at + padded, rows, stride=share)

        for level in range(levels):
            for k in range(tiles):
                def pair(at):
                    lower, upper = (every(at, rows), every(at + 1, rows))
                    return face(field[level, k, lower, :], field[level, k, upper, :], pre[level, k, lower, :], pre[level, k, upper, :])

                low_at, high_at = (rows - 1, late - rows)
                fixed = jac[level, k, every(low_at), :] - kappa[k, every(low_at), :] * (above * pair(low_at))
                work[level, k, pl.ds(g * rows * late + low_at, rows, stride=late), :] = fixed
                fixed = jac[level, k, every(high_at), :] + kappa[k, every(high_at), :] * (below * pair(high_at - 1))
                work[level, k, pl.ds(g * rows * late + high_at, rows, stride=late), :] = fixed

        def one(j, _):
            stencil_tile(
                j, chunks - 2, chunks, field, pre, kappa, scol, aligned, geometry,
                work, "", j * late + rows,
            )
            return 0

        def some(q, _):
            lax.fori_loop(q * GROUP, q * GROUP + GROUP, one, 0)
            for k in range(tiles):
                late_copy(q, k).start()
            return 0

        lax.fori_loop(g * (rows // GROUP), (g + 1) * (rows // GROUP), some, 0)
        return 0

    lax.fori_loop(0, members // rows, group, 0)

    def drain(q, _):
        for k in range(tiles):
            late_copy(q, k).wait()
        return 0

    lax.fori_loop(0, members // GROUP, drain, 0)
    for copy in pre_copies + early_copies:
        copy.wait()


def on_device(bands, members, state, direction, diffusivity, inverses):
    levels, local_rows, width = state.shape
    chunks = inverses.shape[0]
    tiles = width // 128
    share = local_rows // members
    table_hi, table_lo, turns, weights = make_tables()
    geometry = jnp.asarray(make_geometry(bands, members, share))
    f32 = jnp.float32
    anywhere = pl.BlockSpec(memory_space=pl.ANY)
    on_chip = pl.BlockSpec(memory_space=pltpu.VMEM)
    dma = pltpu.SemaphoreType.DMA
    padded = (levels, tiles, local_rows + 16, 128)
    parts = pl.pallas_call(
        functools.partial(exchange_kernel, bands, members, chunks),
        out_shape=(
            pltpu.VMEM(padded, f32),
            pltpu.VMEM(padded, f32),
            pltpu.VMEM((levels, tiles, local_rows, 128), f32),
            pltpu.VMEM((tiles, local_rows, 128), f32),
            pltpu.VMEM((2, levels * 8, 128), f32),
            pltpu.VMEM((members, levels, 8, 128), f32),
            pltpu.VMEM(geometry.shape[1:], f32),
        ),
        in_specs=[pl.BlockSpec(memory_space=pltpu.HBM)] * 9,
        out_specs=(on_chip,) * 7,
        scratch_shapes=[
            pltpu.VMEM((chunks, levels, 8, members * width), f32),
            pltpu.VMEM((chunks, levels, members * tiles, 8, 128), f32),
            pltpu.VMEM(inverses.shape, jnp.bfloat16),
            pltpu.VMEM(table_hi.shape, jnp.bfloat16),
            pltpu.VMEM(table_lo.shape, jnp.bfloat16),
            pltpu.VMEM(turns.shape, f32),
            pltpu.VMEM(weights.shape, f32),
            pltpu.VMEM((tiles, local_rows, 128), jnp.bfloat16),
            pltpu.VMEM((8, levels * 8 * OUTER, 128), f32),
            pltpu.VMEM((levels * 8 * OUTER, 2 * INNER), jnp.bfloat16),
            pltpu.VMEM((levels * 8 * OUTER, 2 * INNER), jnp.bfloat16),
            pltpu.VMEM((levels * 8 * OUTER, INNER), f32),
            pltpu.VMEM((64, OUTER, HALF), f32),
            pltpu.VMEM((2, levels * 8, 128), f32),
            pltpu.VMEM((2, members, levels, 128), f32),
            pltpu.VMEM((4, 16, 128), f32),
            pltpu.VMEM((4, 16, 128), f32),
            pltpu.VMEM((2, members, levels, 128), f32),
            dma((6,)), dma((2 * tiles,)), dma((chunks,)), dma((chunks,)), dma((2,)),
            dma, dma((chunks,)), dma, dma((chunks,)),
            dma((4,)), dma((4,)), dma((2,)), dma((2,)), dma((2,)), dma((2,)),
        ],
        compiler_params=pltpu.CompilerParams(
            collective_id=0, has_side_effects=True, vmem_limit_bytes=LIMIT << 20
        ),
        name="exchange",
    )(
        *[
            pltpu.with_memory_space_constraint(jnp.asarray(x), pltpu.HBM)
            for x in (state, direction, diffusivity, inverses, table_hi, table_lo, turns, weights, geometry)
        ]
    )
    return pl.pallas_call(
        functools.partial(finish_kernel, members, chunks),
        out_shape=(jax.ShapeDtypeStruct(state.shape, f32),) * 2,
        in_specs=[on_chip] * 7,
        out_specs=(anywhere,) * 2,
        scratch_shapes=[
            pltpu.VMEM((levels, tiles, members * 24, 128), f32),
            dma((tiles,)), dma((tiles,)), dma((members // GROUP, tiles)),
        ],
        compiler_params=pltpu.CompilerParams(vmem_limit_bytes=8 << 20),
        name="finish",
    )(*parts)


def solution(mesh):
    return jax.shard_map(
        functools.partial(on_device, mesh.shape["lat"], mesh.shape["lon"]),
        mesh=mesh,
        in_specs=(
            P(None, "lat", "lon"),
            P(None, "lat", "lon"),
            P("lat", "lon"),
            P(("lat", "lon"), None, None, None, None),
        ),
        out_specs=(P(None, "lat", "lon"), P(None, "lat", "lon")),
        check_vma=False,
    )
```
